32 devices in a mesh: group: 2 (over x), dom: 16 (over z, y, core).
Axes of the slice: x: 2, y: 2, z: 4, core: 2. Of those that a mesh axis runs over, the one named last changes fastest.
Arguments:
- features: bfloat16 [8192, 512], P(('group', 'dom')), may hold values from -6 to 6
- tile_columns: int32 [32, 2, 4], P(('group', 'dom')), may hold values from 0 to 1
- tile_values: bfloat16 [32, 2, 4, 128, 128], P(('group', 'dom')), as said below
- send_rows: int32 [32, 16, 16], P(('group', 'dom')), may hold values from 0 to 255
- send_count: int32 [32, 16], P(('group', 'dom')), may hold values from 0 to 16, as said below
- ghost_target: int32 [32, 16, 16], P(('group', 'dom')), may hold values from 0 to 255
- query_rows: int32 [32, 512], P(('group', 'dom')), may hold values from 0 to 255
- positive_cand: int32 [32, 512], P(('group', 'dom')), may hold values from 0 to 63
- negative_rows: int32 [32, 32], P(('group', 'dom')), may hold values from 0 to 255
- weight_self: bfloat16 [512, 512], replicated, may hold values from -0.25 to 0.25
- weight_neigh: bfloat16 [512, 512], replicated, may hold values from -0.75 to 0.75
Outputs:
- embeddings: bfloat16 [8192, 512], P(('group', 'dom'))
- weight_grads: bfloat16 [1024, 512], P('dom')
The draws below stay inside these ranges and needn't reach their ends.
Inputs may be any that keep to these rules, and one draw needn't show every extreme that they name: `send_count`: no device sends rows to its own index of dom; in every group one index of dom receives exactly 16 rows from every other index. `tile_values`: weights are zero or between 0.5 and 1.
All inputs are finite; a program needn't handle non-finite values.
Results may differ from the reference program's by a relative error of at most 0.015.
Values may be sent and summed in bfloat16 or wider, within the bound.
No kernel may reach another device: no remote copies, remote signals or barrier semaphores. Data moves between devices by JAX's collectives and lax.ppermute only.
A program may use at most 64 MiB of HBM per device.

```python
import math
import jax
import jax.numpy as jnp
from jax import lax

D = 512
TILE = 128
TILES_ROW = 4
ROW_BLOCKS = 2
SLOTS = 16
QUERIES = 512
NEGATIVES = 32
NODE_DEV = 256
NODES = 8192
CANDIDATES = 64
N_GROUP = 2
N_DOM = 16
DEVICES = 32


def draw_send_count(key, part):
    key_base, key_full = jax.random.split(key)
    base = jax.random.randint(key_base, (DEVICES, N_DOM), 0, SLOTS + 1)
    full_index = jax.random.randint(key_full, (N_GROUP,), 0, N_DOM)
    full_device = jnp.repeat(full_index, N_DOM)
    column = jnp.arange(N_DOM)[None, :]
    own_index = (jnp.arange(DEVICES) % N_DOM)[:, None]
    counts = jnp.where(column == full_device[:, None], SLOTS, base)
    return jnp.where(column == own_index, 0, counts).astype(jnp.int32)


def draw_tile_values(key, part):
    key_mask, key_value = jax.random.split(key)
    shape = (DEVICES, ROW_BLOCKS, TILES_ROW, TILE, TILE)
    present = jax.random.uniform(key_mask, shape, jnp.float32) < 0.05
    weight = 0.5 + 0.5 * jax.random.uniform(key_value, shape, jnp.float32)
    return jnp.where(present, weight, 0.0).astype(jnp.bfloat16)


def place_ends(values, key, low, largest):
    place = [jax.random.randint(jax.random.fold_in(key, axis), (), 0, length) for axis, length in enumerate(values.shape)]
    widest = values.shape.index(max(values.shape))
    beside = place[:widest] + [(place[widest] + 1) % values.shape[widest]] + place[widest + 1:]
    return values.at[tuple(place)].set(low).at[tuple(beside)].set(largest)


def steps_of(key, extent, shards, low, largest):
    def one(axis_at, shards_of):
        steps = jax.random.uniform(jax.random.fold_in(jax.random.fold_in(key, 6), axis_at), (shards_of,), jnp.float32, low / len(shards), largest / len(shards))
        return jnp.repeat(jnp.exp(steps), extent[axis_at] // shards_of).reshape((-1,) + (1,) * (len(extent) - axis_at - 1))

    level = one(*shards[0])
    for cut in shards[1:]:
        level = level * one(*cut)
    return level


def bell_draw(key, shape, width, bound, cuts=(), kind=jnp.bfloat16):
    loudness = steps_of(key, shape, cuts, -0.22, 0.18) if cuts else 1.0
    result = jax.random.normal(key, shape, jnp.float32) * width * loudness
    return jnp.minimum(jnp.maximum(result, -bound), bound).astype(kind)


def setup_inputs(seed: int = 0) -> dict:
    streams_of = jax.random.split(jax.random.key(seed), 12)
    features = bell_draw(streams_of[0], (NODES, D), 1.0, 6.0, ((0, 32),))
    tile_columns = place_ends(jax.random.randint(streams_of[1], (DEVICES, ROW_BLOCKS, TILES_ROW), 0, ROW_BLOCKS), jax.random.fold_in(streams_of[1], 1), 0, ROW_BLOCKS - 1).astype(jnp.int32)
    tile_values = draw_tile_values(jax.random.fold_in(streams_of[11], 71), 0)
    send_rows = place_ends(jax.random.randint(streams_of[3], (DEVICES, N_DOM, SLOTS), 0, NODE_DEV), jax.random.fold_in(streams_of[3], 1), 0, NODE_DEV - 1).astype(jnp.int32)
    send_count = draw_send_count(jax.random.fold_in(streams_of[11], 71), 0)
    ghost_target = place_ends(jax.random.randint(streams_of[5], (DEVICES, N_DOM, SLOTS), 0, NODE_DEV), jax.random.fold_in(streams_of[5], 1), 0, NODE_DEV - 1).astype(jnp.int32)
    query_rows = place_ends(jax.random.randint(streams_of[6], (DEVICES, QUERIES), 0, NODE_DEV), jax.random.fold_in(streams_of[6], 1), 0, NODE_DEV - 1).astype(jnp.int32)
    positive_cand = place_ends(jax.random.randint(streams_of[7], (DEVICES, QUERIES), 0, CANDIDATES), jax.random.fold_in(streams_of[7], 1), 0, CANDIDATES - 1).astype(jnp.int32)
    negative_rows = place_ends(jax.random.randint(streams_of[8], (DEVICES, NEGATIVES), 0, NODE_DEV), jax.random.fold_in(streams_of[8], 1), 0, NODE_DEV - 1).astype(jnp.int32)
    weight_self = bell_draw(streams_of[9], (D, D), D ** -0.5, 0.25)
    weight_neigh = bell_draw(streams_of[10], (D, D), (D // 9) ** -0.5, 0.75)
    return dict(features=features, tile_columns=tile_columns, tile_values=tile_values, send_rows=send_rows, send_count=send_count, ghost_target=ghost_target, query_rows=query_rows, positive_cand=positive_cand, negative_rows=negative_rows, weight_self=weight_self, weight_neigh=weight_neigh)


LOSS_FACTOR = 64.0
EPSILON = 1e-05

def reference(features, tile_columns, tile_values, send_rows, send_count, ghost_target, query_rows, positive_cand, negative_rows, weight_self, weight_neigh):
    score_factor = 1.0 / math.sqrt(D)
    nodes = features.reshape(DEVICES, NODE_DEV, D)

    def forward(device):
        group_index = device // N_DOM
        dom_index = device % N_DOM
        peers = group_index * N_DOM + jnp.arange(N_DOM, dtype=jnp.int32)
        rows_index = send_rows[peers, dom_index]
        counts = send_count[peers, dom_index]
        ghosts = nodes[peers[:, None], rows_index]
        live = (jnp.arange(SLOTS, dtype=jnp.int32)[None, :] < counts[:, None]).astype(jnp.float32)
        targets = ghost_target[device].reshape(-1)
        weighted = (ghosts.astype(jnp.float32) * live[:, :, None]).reshape(-1, D)
        ghost_sum = jnp.zeros((NODE_DEV, D), jnp.float32).at[targets].add(weighted)
        ghost_count = jnp.zeros((NODE_DEV,), jnp.float32).at[targets].add(live.reshape(-1))
        own = nodes[device]
        blocks = own.reshape(ROW_BLOCKS, TILE, D)
        picked = blocks[tile_columns[device]]
        tiles = tile_values[device].astype(jnp.float32)
        local = jnp.einsum('rtij,rtjd->rid', tiles, picked.astype(jnp.float32)).reshape(NODE_DEV, D)
        degree = 1.0 + lax.optimization_barrier(jnp.sum(tiles, axis=(1, 3))).reshape(NODE_DEV) + ghost_count
        aggregate = ((local + ghost_sum) / degree[:, None]).astype(jnp.bfloat16)
        pre = jnp.dot(own, weight_self, preferred_element_type=jnp.float32) + jnp.dot(aggregate, weight_neigh, preferred_element_type=jnp.float32)
        scale = lax.rsqrt(lax.optimization_barrier(jnp.mean(pre * pre, axis=-1, keepdims=True)) + EPSILON)
        return ((pre * scale).astype(jnp.bfloat16), aggregate)
    embeds, aggregates = lax.map(forward, jnp.arange(DEVICES, dtype=jnp.int32))

    def device_grad(owner, query_grad, cand_grad):
        emb_grad = jnp.zeros((NODE_DEV, D), jnp.float32)
        emb_grad = emb_grad.at[query_rows[owner]].add(query_grad)
        emb_grad = emb_grad.at[negative_rows[owner]].add(cand_grad)
        own = nodes[owner]
        aggregate = aggregates[owner]
        pre = jnp.dot(own, weight_self, preferred_element_type=jnp.float32) + jnp.dot(aggregate, weight_neigh, preferred_element_type=jnp.float32)
        scale = lax.rsqrt(lax.optimization_barrier(jnp.mean(pre * pre, axis=-1, keepdims=True)) + EPSILON)
        inner = lax.optimization_barrier(jnp.mean(pre * emb_grad, axis=-1, keepdims=True))
        pre_grad = (scale * emb_grad - pre * scale * scale * scale * inner).astype(jnp.bfloat16)
        stacked = jnp.concatenate([own, aggregate], axis=1)
        return jnp.dot(stacked.T, pre_grad, preferred_element_type=jnp.float32)

    def backward(total, dom_index):
        owners = jnp.arange(N_GROUP, dtype=jnp.int32) * N_DOM + dom_index
        cands = embeds[owners[:, None], negative_rows[owners]].reshape(CANDIDATES, D)
        queries = embeds[owners[:, None], query_rows[owners]]
        score = score_factor * jnp.einsum('gqd,cd->gqc', queries.astype(jnp.float32), cands.astype(jnp.float32))
        positive = positive_cand[owners][:, :, None] == jnp.arange(CANDIDATES, dtype=jnp.int32)[None, None, :]
        sigma = jax.nn.sigmoid(score)
        dscore = jnp.where(positive, sigma - 1.0, sigma / (CANDIDATES - 1.0)) * (LOSS_FACTOR / QUERIES)
        dscore = dscore.astype(jnp.bfloat16).astype(jnp.float32)
        query_grad = score_factor * jnp.einsum('gqc,cd->gqd', dscore, cands.astype(jnp.float32))
        cand_grad = score_factor * jnp.einsum('gqc,gqd->cd', dscore, queries.astype(jnp.float32))
        grads = jax.vmap(device_grad)(owners, query_grad, cand_grad.reshape(N_GROUP, NEGATIVES, D))
        return (total + lax.optimization_barrier(jnp.sum(grads, axis=0)), None)
    total, unused = lax.scan(backward, jnp.zeros((2 * D, D), jnp.float32), jnp.arange(N_DOM, dtype=jnp.int32))
    return (embeds.reshape(NODES, D), total.astype(jnp.bfloat16))
```

```python
import functools
import math

import jax
import jax.numpy as jnp
from jax import lax
from jax.experimental import pallas as pl
from jax.experimental.pallas import tpu as pltpu
from jax.sharding import PartitionSpec as P

LOSS_FACTOR = 64.0
EPSILON = 1e-05
DEAD = 256.0
DEAD_FLOOR = 128.0

F32 = jnp.float32
BF16 = jnp.bfloat16


def iota(shape, axis):
    return lax.broadcasted_iota(jnp.int32, shape, axis)


def dot(left, right, left_axis=1, right_axis=0):
    return lax.dot_general(
        left, right, (((left_axis,), (right_axis,)), ((), ())), preferred_element_type=F32
    )


def one_hot(condition):
    return jnp.where(condition, 1.0, 0.0).astype(BF16)


def slot_selector(peers, slots):
    shape = (peers * slots, peers)
    row, peer = iota(shape, 0), iota(shape, 1)
    mine = (row >= peer * slots) & (row < (peer + 1) * slots)
    first = jnp.sum(jnp.where(mine, (peer * slots).astype(F32), 0.0), axis=1, keepdims=True)
    return mine, row[:, :1].astype(F32) - first


def pack_kernel(rows_ref, count_ref, x_ref, out_ref):
    peers, slots = rows_ref.shape[1:]
    nodes = x_ref.shape[0]
    total = peers * slots
    mine, place = slot_selector(peers, slots)
    table = dot(one_hot(mine), rows_ref[0].astype(F32).astype(BF16))
    at_place = iota((total, slots), 1).astype(F32) == place
    row = jnp.sum(jnp.where(at_place, table, 0.0), axis=1, keepdims=True)
    count = jnp.sum(jnp.where(mine, count_ref[...].astype(F32), 0.0), axis=1, keepdims=True)
    pick = one_hot(iota((total, nodes), 1).astype(F32) == row)
    out = dot(pick, x_ref[...])
    out_ref[...] = jnp.where(place < count, out, DEAD).astype(BF16)


def local_kernel(
    columns_ref,
    group_ref,
    values_ref,
    x_ref,
    weight_self_ref,
    target_ref,
    query_ref,
    positive_ref,
    negative_ref,
    local_ref,
    degree_ref,
    self_ref,
    pair_ref,
    target_hot_ref,
    negative_hot_ref,
    x_negative_ref,
    x_turned_ref,
):
    row_blocks, tiles_row, tile = values_ref.shape[1:4]
    nodes = x_ref.shape[0]
    peers, slots = target_ref.shape[1:]
    negatives = negative_ref.shape[1]
    queries = query_ref.shape[1]
    candidates = pair_ref.shape[1]

    relative = positive_ref[...] - group_ref[0] * negatives
    relative = jnp.where(relative < 0, relative + candidates, relative)
    query_hot = one_hot(iota((nodes, queries), 0) == query_ref[...])
    positive_hot = one_hot(iota((candidates, queries), 0) == relative)
    pair_ref[...] = dot(query_hot, positive_hot, 1, 1)

    square = (negatives, negatives)
    negative = jnp.sum(
        jnp.where(iota(square, 0) == iota(square, 1), negative_ref[...].astype(F32), 0.0),
        axis=1,
        keepdims=True,
    )
    negative_hot = one_hot(iota((negatives, nodes), 1).astype(F32) == negative)
    negative_hot_ref[...] = negative_hot
    x_negative_ref[...] = dot(negative_hot, x_ref[...]).astype(BF16)

    ones = jnp.ones((tile, 128), BF16)
    for block in range(row_blocks):
        total = jnp.zeros((tile, x_ref.shape[1]), F32)
        weight = jnp.ones((tile, 128), F32)
        for t in range(tiles_row):
            first = pl.multiple_of(columns_ref[0, block, t] * tile, tile)
            values = values_ref[0, block, t]
            total += dot(values, x_ref[pl.ds(first, tile), :])
            weight += dot(values, ones)
        local_ref[block * tile : (block + 1) * tile, :] = total
        degree_ref[block * tile : (block + 1) * tile, :] = weight

    self_ref[...] = dot(x_ref[...], weight_self_ref[...])
    x_turned_ref[...] = x_ref[...].T.reshape(x_turned_ref.shape)

    total = peers * slots
    shape = (peers, total)
    peer, column = iota(shape, 0), iota(shape, 1)
    mine = (column >= peer * slots) & (column < (peer + 1) * slots)
    first = jnp.sum(jnp.where(mine, (peer * slots).astype(F32), 0.0), axis=0, keepdims=True)
    place = iota((1, total), 1).astype(F32) - first
    spread = one_hot(iota((slots, total), 0).astype(F32) == place)
    table = dot(target_ref[0].astype(F32).astype(BF16), spread)
    target = jnp.sum(jnp.where(mine, table, 0.0), axis=0, keepdims=True)
    target_hot_ref[...] = one_hot(iota((nodes, total), 0).astype(F32) == target)


def aggregate_kernel(
    received_ref, target_hot_ref, local_ref, degree_ref, negative_hot_ref, out_ref, negative_ref
):
    received = received_ref[...].astype(F32)
    live = received[:, :1] < DEAD_FLOOR
    weighted = jnp.where(live, received, 0.0).astype(BF16)
    flags = jnp.broadcast_to(jnp.where(live, 1.0, 0.0), (received.shape[0], 128)).astype(BF16)
    hot = target_hot_ref[...]
    degree = degree_ref[...] + dot(hot, flags)
    summed = local_ref[...] + dot(hot, weighted)
    width = summed.shape[1]
    for first in range(0, width, 128):
        out_ref[:, first : first + 128] = (summed[:, first : first + 128] / degree).astype(BF16)
    negative_ref[...] = dot(negative_hot_ref[...], out_ref[...]).astype(BF16)


def embed_kernel(
    self_ref, aggregate_ref, weight_neigh_ref, embeds_ref, exact_ref, scale_ref, turned_ref
):
    aggregate = aggregate_ref[...]
    pre = self_ref[...] + dot(aggregate, weight_neigh_ref[...])
    scale = lax.rsqrt(jnp.mean(pre * pre, axis=1, keepdims=True) + EPSILON)
    exact = pre * scale
    exact_ref[...] = exact
    embeds_ref[...] = exact.astype(BF16)
    scale_ref[...] = jnp.broadcast_to(scale, scale_ref.shape)
    turned_ref[...] = aggregate.T.reshape(turned_ref.shape)


def split_dot(left, right, left_axis):
    high = left.astype(BF16)
    low = (left - high.astype(F32)).astype(BF16)
    return dot(high, right, left_axis, 0) + dot(low, right, left_axis, 0)


def gradient_kernel(
    query_total,
    core_ref,
    x_cand_ref,
    aggregate_cand_ref,
    weight_self_ref,
    weight_neigh_ref,
    embeds_ref,
    exact_ref,
    scale_ref,
    pair_ref,
    x_turned_ref,
    aggregate_turned_ref,
    keep_ref,
    send_ref,
    x_cand_turned_ref,
    aggregate_cand_turned_ref,
):
    width = embeds_ref.shape[1]
    score_factor = 1.0 / math.sqrt(width)
    candidates = x_cand_ref.shape[0]

    x_cand, aggregate_cand = x_cand_ref[...], aggregate_cand_ref[...]
    pre = dot(x_cand, weight_self_ref[...]) + dot(aggregate_cand, weight_neigh_ref[...])
    scale_cand = lax.rsqrt(jnp.mean(pre * pre, axis=1, keepdims=True) + EPSILON)
    exact_cand = pre * scale_cand
    cand = exact_cand.astype(BF16)

    embeds = embeds_ref[...]
    scores = score_factor * dot(embeds, cand, 1, 1)
    sigma = jax.nn.sigmoid(scores)
    factor = LOSS_FACTOR / query_total
    at_positive = ((sigma - 1.0) * factor).astype(BF16).astype(F32)
    elsewhere = ((sigma / (candidates - 1.0)) * factor).astype(BF16).astype(F32)
    pair = pair_ref[...]
    count = jnp.sum(pair, axis=1, keepdims=True)
    grad = (count - pair) * elsewhere + pair * at_positive

    emb_grad = score_factor * split_dot(grad, cand, 1)
    cand_grad = score_factor * split_dot(grad, embeds, 0)

    def through_norm(given, exact, scale):
        inner = jnp.mean(exact * given, axis=1, keepdims=True)
        return (scale * (given - exact * inner)).astype(BF16)

    pre_grad = through_norm(emb_grad, exact_ref[...], scale_ref[:, :1])
    pre_grad_cand = through_norm(cand_grad, exact_cand, scale_cand)

    half, _, rows, _ = x_turned_ref.shape
    x_cand_turned_ref[...] = x_cand.T.reshape(half, 2, rows, candidates)
    aggregate_cand_turned_ref[...] = aggregate_cand.T.reshape(half, 2, rows, candidates)
    own = core_ref[0]
    parts = (
        (x_turned_ref, x_cand_turned_ref),
        (aggregate_turned_ref, aggregate_cand_turned_ref),
    )
    for ref, core in ((send_ref, 1 - own), (keep_ref, own)):
        for part, (turned_ref, cand_turned_ref) in enumerate(parts):
            left = turned_ref[:, core].reshape(half * rows, turned_ref.shape[3])
            left_cand = cand_turned_ref[:, core].reshape(half * rows, candidates)
            block = dot(left, pre_grad) + dot(left_cand, pre_grad_cand)
            ref[part * half : (part + 1) * half] = block.reshape(half, rows, width).astype(BF16)


VMEM = pl.BlockSpec(memory_space=pltpu.VMEM)
SMEM = pl.BlockSpec(memory_space=pltpu.SMEM)


def call(kernel, name, outs, args, scalars=0, flops=0, scratch=()):
    shapes = [jax.ShapeDtypeStruct(shape, kind) for shape, kind in outs]
    moved = sum(math.prod(a.shape) * a.dtype.itemsize for a in list(args) + shapes)
    return pl.pallas_call(
        kernel,
        name=name,
        out_shape=shapes,
        in_specs=[SMEM] * scalars + [VMEM] * (len(args) - scalars),
        out_specs=[VMEM] * len(outs),
        scratch_shapes=[pltpu.VMEM(shape, kind) for shape, kind in scratch],
        cost_estimate=pl.CostEstimate(flops=flops, bytes_accessed=moved, transcendentals=0),
    )(*args)


def on_device(
    features,
    tile_columns,
    tile_values,
    send_rows,
    send_count,
    ghost_target,
    query_rows,
    positive_cand,
    negative_rows,
    weight_self,
    weight_neigh,
):
    nodes, width = features.shape
    peers, slots = send_rows.shape[1:]
    total = peers * slots
    negatives = negative_rows.shape[1]
    groups = lax.axis_size("group")
    candidates = negatives * groups
    chips = peers // 2
    rows = 2 * width // peers
    half = chips // 2
    group = lax.axis_index("group").astype(jnp.int32).reshape(1)
    core = (lax.axis_index("dom") % 2).astype(jnp.int32).reshape(1)

    (outgoing,) = call(
        pack_kernel,
        "pack",
        [((total, width), BF16)],
        [send_rows, send_count, features],
        flops=2 * total * nodes * width,
    )
    received = lax.all_to_all(
        outgoing.reshape(peers, slots, width), "dom", split_axis=0, concat_axis=0, tiled=True
    ).reshape(total, width)

    local, degree, own_pre, pair, target_hot, negative_hot, x_negative, x_turned = call(
        local_kernel,
        "local",
        [
            ((nodes, width), F32),
            ((nodes, 128), F32),
            ((nodes, width), F32),
            ((nodes, candidates), F32),
            ((nodes, total), BF16),
            ((negatives, nodes), BF16),
            ((negatives, width), BF16),
            ((half, 2, rows, nodes), BF16),
        ],
        [
            tile_columns,
            group,
            tile_values,
            features,
            weight_self,
            ghost_target,
            query_rows,
            positive_cand,
            negative_rows,
        ],
        scalars=2,
        flops=2 * nodes * width * (width + tile_values.shape[2] * tile_values.shape[3]),
    )

    def gathered(own):
        blocks = [own]
        for k in range(1, groups):
            pairs = [((g + k) % groups, g) for g in range(groups)]
            blocks.append(lax.ppermute(own, "group", pairs))
        return jnp.concatenate(blocks, axis=0)

    x_cand = gathered(x_negative)
    aggregate, aggregate_negative = call(
        aggregate_kernel,
        "aggregate",
        [((nodes, width), BF16), ((negatives, width), BF16)],
        [received, target_hot, local, degree, negative_hot],
        flops=2 * nodes * total * width,
    )
    aggregate_cand = gathered(aggregate_negative)
    embeds, exact, scale, aggregate_turned = call(
        embed_kernel,
        "embed",
        [
            ((nodes, width), BF16),
            ((nodes, width), F32),
            ((nodes, 128), F32),
            ((half, 2, rows, nodes), BF16),
        ],
        [own_pre, aggregate, weight_neigh],
        flops=2 * nodes * width * width,
    )
    keep, send = call(
        functools.partial(gradient_kernel, query_rows.shape[1]),
        "gradient",
        [((chips, rows, width), BF16)] * 2,
        [
            core,
            x_cand,
            aggregate_cand,
            weight_self,
            weight_neigh,
            embeds,
            exact,
            scale,
            pair,
            x_turned,
            aggregate_turned,
        ],
        scalars=1,
        flops=4 * nodes * width * width,
        scratch=[((half, 2, rows, candidates), BF16)] * 2,
    )

    swap = [(i, i ^ 1) for i in range(peers)]
    chip_sum = (keep.astype(F32) + lax.ppermute(send, "dom", swap).astype(F32)).astype(BF16)
    same_core = [[c + 2 * chip for chip in range(chips)] for c in range(2)]
    parts = lax.all_to_all(
        chip_sum,
        "dom",
        split_axis=0,
        concat_axis=0,
        axis_index_groups=same_core,
        tiled=True,
    )
    shard = jnp.sum(parts.astype(F32), axis=0).astype(BF16)
    if groups == 2:
        other = lax.ppermute(shard, "group", [(0, 1), (1, 0)])
        summed = (shard.astype(F32) + other.astype(F32)).astype(BF16)
    else:
        summed = lax.psum(shard, "group")
    return (embeds, summed)


def solution(mesh):
    placed = (
        P(("group", "dom"), None),
        P(("group", "dom"), None, None),
        P(("group", "dom"), None, None, None, None),
        P(("group", "dom"), None, None),
        P(("group", "dom"), None),
        P(("group", "dom"), None, None),
        P(("group", "dom"), None),
        P(("group", "dom"), None),
        P(("group", "dom"), None),
        P(),
        P(),
    )
    return jax.shard_map(
        on_device,
        mesh=mesh,
        in_specs=placed,
        out_specs=(P(("group", "dom"), None), P("dom", None)),
        check_vma=False,
    )
```

```python
import functools
import math

import jax
import jax.numpy as jnp
from jax import lax
from jax.experimental import pallas as pl
from jax.experimental.pallas import tpu as pltpu
from jax.sharding import PartitionSpec as P

LOSS_FACTOR = 64.0
EPSILON = 1e-05
DEAD = 256.0
DEAD_FLOOR = 128.0

F32 = jnp.float32
BF16 = jnp.bfloat16


def iota(shape, axis):
    return lax.broadcasted_iota(jnp.int32, shape, axis)


def dot(left, right, left_axis=1, right_axis=0):
    return lax.dot_general(
        left, right, (((left_axis,), (right_axis,)), ((), ())), preferred_element_type=F32
    )


def one_hot(condition):
    return jnp.where(condition, 1.0, 0.0).astype(BF16)


def pack_kernel(core_ref, rows_hbm, count_hbm, x_hbm, keep_ref, send_ref, rows_ref, count_ref, x_ref, sems):
    copies = [
        pltpu.make_async_copy(source, target, sems.at[n])
        for n, (source, target) in enumerate(
            ((rows_hbm, rows_ref), (count_hbm, count_ref), (x_hbm, x_ref))
        )
    ]
    for copy in copies:
        copy.start()
    peers, slots = rows_ref.shape[1:]
    nodes = x_ref.shape[0]
    half = peers // 2 * slots
    shape = (half, peers)
    row, peer = iota(shape, 0), iota(shape, 1)
    first = (peer >> 1) * slots
    chip = (row >= first) & (row < first + slots)
    copies[0].wait()
    copies[1].wait()
    rows = rows_ref[0].astype(F32).astype(BF16)
    counts = count_ref[...].astype(F32)
    picks = []
    for core in (core_ref[0], 1 - core_ref[0]):
        mine = chip & ((peer & 1) == core)
        start = jnp.sum(jnp.where(mine, first.astype(F32), 0.0), axis=1, keepdims=True)
        place = row[:, :1].astype(F32) - start
        at_place = iota((half, slots), 1).astype(F32) == place
        table = dot(one_hot(mine), rows)
        index = jnp.sum(jnp.where(at_place, table, 0.0), axis=1, keepdims=True)
        count = jnp.sum(jnp.where(mine, counts, 0.0), axis=1, keepdims=True)
        pick = one_hot(iota((half, nodes), 1).astype(F32) == index)
        picks.append((pick, place < count))
    copies[2].wait()
    x = x_ref[...]
    for (pick, live), ref in reversed(list(zip(picks, (keep_ref, send_ref)))):
        ref[...] = jnp.where(live, dot(pick, x), DEAD).astype(BF16).reshape(ref.shape)


def local_kernel(
    columns_ref,
    place_ref,
    values_ref,
    x_ref,
    weight_self_ref,
    target_ref,
    query_ref,
    positive_ref,
    negative_ref,
    local_ref,
    degree_ref,
    self_ref,
    pair_ref,
    target_hot_ref,
    negative_hot_ref,
    x_negative_ref,
    x_turned_ref,
):
    row_blocks, tiles_row, tile = values_ref.shape[1:4]
    nodes = x_ref.shape[0]
    peers, slots = target_ref.shape[1:]
    negatives = negative_ref.shape[1]
    queries = query_ref.shape[1]
    candidates = pair_ref.shape[1]

    relative = positive_ref[...] - place_ref[0] * negatives
    relative = jnp.where(relative < 0, relative + candidates, relative)
    query_hot = one_hot(iota((nodes, queries), 0) == query_ref[...])
    positive_hot = one_hot(iota((candidates, queries), 0) == relative)
    pair_ref[...] = dot(query_hot, positive_hot, 1, 1)

    square = (negatives, negatives)
    negative = jnp.sum(
        jnp.where(iota(square, 0) == iota(square, 1), negative_ref[...].astype(F32), 0.0),
        axis=1,
        keepdims=True,
    )
    negative_hot = one_hot(iota((negatives, nodes), 1).astype(F32) == negative)
    negative_hot_ref[...] = negative_hot
    x_negative_ref[...] = dot(negative_hot, x_ref[...]).astype(BF16)

    ones = jnp.ones((tile, 128), BF16)
    for block in range(row_blocks):
        total = jnp.zeros((tile, x_ref.shape[1]), F32)
        weight = jnp.ones((tile, 128), F32)
        for t in range(tiles_row):
            first = pl.multiple_of(columns_ref[0, block, t] * tile, tile)
            values = values_ref[0, block, t]
            total += dot(values, x_ref[pl.ds(first, tile), :])
            weight += dot(values, ones)
        local_ref[block * tile : (block + 1) * tile, :] = total
        degree_ref[block * tile : (block + 1) * tile, :] = weight

    self_ref[...] = dot(x_ref[...], weight_self_ref[...])
    x_turned_ref[...] = x_ref[...].T.reshape(x_turned_ref.shape)

    total = peers * slots
    shape = (peers, total)
    column = iota(shape, 1)
    start = (iota(shape, 0) ^ place_ref[1]) * slots
    mine = (column >= start) & (column < start + slots)
    first = jnp.sum(jnp.where(mine, start.astype(F32), 0.0), axis=0, keepdims=True)
    place = iota((1, total), 1).astype(F32) - first
    spread = one_hot(iota((slots, total), 0).astype(F32) == place)
    table = dot(target_ref[0].astype(F32).astype(BF16), spread)
    target = jnp.sum(jnp.where(mine, table, 0.0), axis=0, keepdims=True)
    target_hot_ref[...] = one_hot(iota((nodes, total), 0).astype(F32) == target)


def aggregate_kernel(
    received_ref,
    target_hot_ref,
    local_ref,
    degree_ref,
    negative_hot_ref,
    x_negative_ref,
    out_ref,
    negative_ref,
):
    received = received_ref[...].astype(F32)
    live = received[:, :1] < DEAD_FLOOR
    weighted = jnp.where(live, received, 0.0).astype(BF16)
    flags = jnp.broadcast_to(jnp.where(live, 1.0, 0.0), (received.shape[0], 128)).astype(BF16)
    hot = target_hot_ref[...]
    degree = degree_ref[...] + dot(hot, flags)
    summed = local_ref[...] + dot(hot, weighted)
    width = summed.shape[1]
    for first in range(0, width, 128):
        out_ref[:, first : first + 128] = (summed[:, first : first + 128] / degree).astype(BF16)
    negative_ref[0] = x_negative_ref[...]
    negative_ref[1] = dot(negative_hot_ref[...], out_ref[...]).astype(BF16)


def embed_kernel(
    self_ref,
    aggregate_ref,
    weight_neigh_ref,
    embeds_hbm,
    embeds_ref,
    exact_ref,
    scale_ref,
    turned_ref,
    sem,
):
    aggregate = aggregate_ref[...]
    pre = self_ref[...] + dot(aggregate, weight_neigh_ref[...])
    scale = lax.rsqrt(jnp.mean(pre * pre, axis=1, keepdims=True) + EPSILON)
    exact = pre * scale
    embeds_ref[...] = exact.astype(BF16)
    copy = pltpu.make_async_copy(embeds_ref, embeds_hbm, sem)
    copy.start()
    exact_ref[...] = exact
    scale_ref[...] = jnp.broadcast_to(scale, scale_ref.shape)
    turned_ref[...] = aggregate.T.reshape(turned_ref.shape)
    copy.wait()


def split_dot(left, right, left_axis):
    high = left.astype(BF16)
    low = (left - high.astype(F32)).astype(BF16)
    return dot(high, right, left_axis, 0) + dot(low, right, left_axis, 0)


def gradient_kernel(
    query_total,
    core_ref,
    cand_ref,
    weight_self_ref,
    weight_neigh_ref,
    embeds_ref,
    exact_ref,
    scale_ref,
    pair_ref,
    x_turned_ref,
    aggregate_turned_ref,
    keep_ref,
    send_ref,
    x_cand_turned_ref,
    aggregate_cand_turned_ref,
):
    width = embeds_ref.shape[1]
    score_factor = 1.0 / math.sqrt(width)
    candidates = cand_ref.shape[1]

    x_cand, aggregate_cand = cand_ref[0], cand_ref[1]
    pre = dot(x_cand, weight_self_ref[...]) + dot(aggregate_cand, weight_neigh_ref[...])
    scale_cand = lax.rsqrt(jnp.mean(pre * pre, axis=1, keepdims=True) + EPSILON)
    exact_cand = pre * scale_cand
    cand = exact_cand.astype(BF16)

    embeds = embeds_ref[...]
    scores = score_factor * dot(embeds, cand, 1, 1)
    sigma = jax.nn.sigmoid(scores)
    factor = LOSS_FACTOR / query_total
    at_positive = ((sigma - 1.0) * factor).astype(BF16).astype(F32)
    elsewhere = ((sigma / (candidates - 1.0)) * factor).astype(BF16).astype(F32)
    pair = pair_ref[...]
    count = jnp.sum(pair, axis=1, keepdims=True)
    grad = (count - pair) * elsewhere + pair * at_positive

    emb_grad = score_factor * split_dot(grad, cand, 1)
    cand_grad = score_factor * split_dot(grad, embeds, 0)

    def through_norm(given, exact, scale):
        inner = jnp.mean(exact * given, axis=1, keepdims=True)
        return (scale * (given - exact * inner)).astype(BF16)

    pre_grad = through_norm(emb_grad, exact_ref[...], scale_ref[:, :1])
    pre_grad_cand = through_norm(cand_grad, exact_cand, scale_cand)

    half, _, rows, _ = x_turned_ref.shape
    x_cand_turned_ref[...] = x_cand.T.reshape(half, 2, rows, candidates)
    aggregate_cand_turned_ref[...] = aggregate_cand.T.reshape(half, 2, rows, candidates)
    own = core_ref[0]
    parts = (
        (x_turned_ref, x_cand_turned_ref),
        (aggregate_turned_ref, aggregate_cand_turned_ref),
    )
    for ref, core in ((send_ref, 1 - own), (keep_ref, own)):
        for part, (turned_ref, cand_turned_ref) in enumerate(parts):
            left = turned_ref[:, core].reshape(half * rows, turned_ref.shape[3])
            left_cand = cand_turned_ref[:, core].reshape(half * rows, candidates)
            block = dot(left, pre_grad) + dot(left_cand, pre_grad_cand)
            ref[part * half : (part + 1) * half] = block.reshape(half, rows, width).astype(BF16)


VMEM = pl.BlockSpec(memory_space=pltpu.VMEM)
SMEM = pl.BlockSpec(memory_space=pltpu.SMEM)
HBM = pl.BlockSpec(memory_space=pltpu.HBM)


def call(kernel, name, outs, args, flops=0, scratch=()):
    shapes = [jax.ShapeDtypeStruct(shape, kind) for shape, kind, _ in outs]
    arrays = [a for a, _ in args]
    moved = sum(math.prod(a.shape) * a.dtype.itemsize for a in arrays + shapes)
    return pl.pallas_call(
        kernel,
        name=name,
        out_shape=shapes,
        in_specs=[place for _, place in args],
        out_specs=[place for _, _, place in outs],
        scratch_shapes=list(scratch),
        compiler_params=pltpu.CompilerParams(vmem_limit_bytes=16 << 20),
        cost_estimate=pl.CostEstimate(flops=flops, bytes_accessed=moved, transcendentals=0),
    )(*arrays)


def on_device(
    features,
    tile_columns,
    tile_values,
    send_rows,
    send_count,
    ghost_target,
    query_rows,
    positive_cand,
    negative_rows,
    weight_self,
    weight_neigh,
):
    nodes, width = features.shape
    peers, slots = send_rows.shape[1:]
    total = peers * slots
    negatives = negative_rows.shape[1]
    groups = lax.axis_size("group")
    candidates = negatives * groups
    chips = peers // 2
    rows = 2 * width // peers
    half = chips // 2
    group = lax.axis_index("group").astype(jnp.int32)
    core = (lax.axis_index("dom") & 1).astype(jnp.int32)
    swap = [(i, i ^ 1) for i in range(peers)]
    same_core = [[c + 2 * chip for chip in range(chips)] for c in range(2)]

    keep, send = call(
        pack_kernel,
        "pack",
        [((chips, slots, width), BF16, VMEM)] * 2,
        [(core.reshape(1), SMEM), (send_rows, HBM), (send_count, HBM), (features, HBM)],
        flops=2 * total * nodes * width,
        scratch=[
            pltpu.VMEM(send_rows.shape, jnp.int32),
            pltpu.VMEM(send_count.shape, jnp.int32),
            pltpu.VMEM(features.shape, BF16),
            pltpu.SemaphoreType.DMA((3,)),
        ],
    )
    swapped = lax.ppermute(send, "dom", swap)
    local, degree, own_pre, pair, target_hot, negative_hot, x_negative, x_turned = call(
        local_kernel,
        "local",
        [
            ((nodes, width), F32, VMEM),
            ((nodes, 128), F32, VMEM),
            ((nodes, width), F32, VMEM),
            ((nodes, candidates), F32, VMEM),
            ((nodes, total), BF16, VMEM),
            ((negatives, nodes), BF16, VMEM),
            ((negatives, width), BF16, VMEM),
            ((half, 2, rows, nodes), BF16, VMEM),
        ],
        [
            (tile_columns, SMEM),
            (jnp.stack([group, core]), SMEM),
            (tile_values, VMEM),
            (features, VMEM),
            (weight_self, VMEM),
            (ghost_target, VMEM),
            (query_rows, VMEM),
            (positive_cand, VMEM),
            (negative_rows, VMEM),
        ],
        flops=2 * nodes * width * (width + tile_values.shape[2] * tile_values.shape[3]),
    )
    swapped, local = lax.optimization_barrier((swapped, local))
    received = lax.all_to_all(
        jnp.concatenate([keep, swapped], axis=1),
        "dom",
        split_axis=0,
        concat_axis=0,
        axis_index_groups=same_core,
        tiled=True,
    ).reshape(total, width)

    aggregate, own_cand = call(
        aggregate_kernel,
        "aggregate",
        [((nodes, width), BF16, VMEM), ((2, negatives, width), BF16, VMEM)],
        [
            (a, VMEM)
            for a in (received, target_hot, local, degree, negative_hot, x_negative)
        ],
        flops=2 * nodes * total * width,
    )
    cand = [own_cand]
    for k in range(1, groups):
        cand.append(
            lax.ppermute(own_cand, "group", [((g + k) % groups, g) for g in range(groups)])
        )
    embeds_out, embeds, exact, scale, aggregate_turned = call(
        embed_kernel,
        "embed",
        [
            ((nodes, width), BF16, HBM),
            ((nodes, width), BF16, VMEM),
            ((nodes, width), F32, VMEM),
            ((nodes, 128), F32, VMEM),
            ((half, 2, rows, nodes), BF16, VMEM),
        ],
        [(own_pre, VMEM), (aggregate, VMEM), (weight_neigh, VMEM)],
        flops=2 * nodes * width * width,
        scratch=[pltpu.SemaphoreType.DMA],
    )
    keep, send = call(
        functools.partial(gradient_kernel, query_rows.shape[1]),
        "gradient",
        [((chips, rows, width), BF16, VMEM)] * 2,
        [(core.reshape(1), SMEM)]
        + [
            (a, VMEM)
            for a in (
                jnp.concatenate(cand, axis=1),
                weight_self,
                weight_neigh,
                embeds,
                exact,
                scale,
                pair,
                x_turned,
                aggregate_turned,
            )
        ],
        flops=4 * nodes * width * width,
        scratch=[pltpu.VMEM((half, 2, rows, candidates), BF16)] * 2,
    )

    part = rows // groups
    chip_sum = (keep.astype(F32) + lax.ppermute(send, "dom", swap).astype(F32)).astype(BF16)
    all_chips = [
        [g * peers + 2 * chip + c for chip in range(chips) for g in range(groups)]
        for c in range(2)
    ]
    parts = lax.all_to_all(
        chip_sum.reshape(chips * groups, part, width),
        ("group", "dom"),
        split_axis=0,
        concat_axis=0,
        axis_index_groups=all_chips,
        tiled=True,
    )
    summed = jnp.sum(parts.astype(F32), axis=0).astype(BF16)
    if groups == 2:
        other = lax.ppermute(summed, "group", [(0, 1), (1, 0)])
        shard = jnp.where(
            group == 0,
            jnp.concatenate([summed, other], axis=0),
            jnp.concatenate([other, summed], axis=0),
        )
    else:
        shard = lax.all_gather(summed, "group", axis=0, tiled=True)
    return (embeds_out, shard)


def solution(mesh):
    placed = (
        P(("group", "dom"), None),
        P(("group", "dom"), None, None),
        P(("group", "dom"), None, None, None, None),
        P(("group", "dom"), None, None),
        P(("group", "dom"), None),
        P(("group", "dom"), None, None),
        P(("group", "dom"), None),
        P(("group", "dom"), None),
        P(("group", "dom"), None),
        P(),
        P(),
    )
    return jax.shard_map(
        on_device,
        mesh=mesh,
        in_specs=placed,
        out_specs=(P(("group", "dom"), None), P("dom", None)),
        check_vma=False,
    )
```

```python
import functools
import math

import jax
import jax.numpy as jnp
from jax import lax
from jax.experimental import pallas as pl
from jax.experimental.pallas import tpu as pltpu
from jax.sharding import PartitionSpec as P

LOSS_FACTOR = 64.0
EPSILON = 1e-05
DEAD = 256.0
DEAD_FLOOR = 128.0

F32 = jnp.float32
BF16 = jnp.bfloat16


def iota(shape, axis):
    return lax.broadcasted_iota(jnp.int32, shape, axis)


def dot(left, right, left_axis=1, right_axis=0):
    return lax.dot_general(
        left, right, (((left_axis,), (right_axis,)), ((), ())), preferred_element_type=F32
    )


def one_hot(condition):
    return jnp.where(condition, 1.0, 0.0).astype(BF16)


def pack_kernel(rows_hbm, count_hbm, x_hbm, out_hbm, rows_ref, count_ref, x_ref, out_ref, sems):
    places = ((rows_hbm, rows_ref), (count_hbm, count_ref), (x_hbm, x_ref))
    loads = [pltpu.make_async_copy(*pair, sems.at[n]) for n, pair in enumerate(places)]
    for load in loads:
        load.start()
    peers, slots = rows_ref.shape[1:]
    nodes, width = x_ref.shape
    total = peers * slots
    row, first = iota((total, peers), 0), iota((total, peers), 1) * slots
    mine = (row >= first) & (row < first + slots)
    start = jnp.sum(jnp.where(mine, first.astype(F32), 0.0), axis=1, keepdims=True)
    place = row[:, :1].astype(F32) - start
    at_place = iota((total, slots), 1).astype(F32) == place
    peer = one_hot(mine)
    loads[0].wait()
    loads[1].wait()
    table = dot(peer, rows_ref[0].astype(F32).astype(BF16))
    index = jnp.sum(jnp.where(at_place, table, 0.0), axis=1, keepdims=True)
    count = jnp.sum(jnp.where(mine, count_ref[...].astype(F32), 0.0), axis=1, keepdims=True)
    live = place < count
    pick = one_hot(iota((total, nodes), 1).astype(F32) == index)
    loads[2].wait()
    stores = []
    part = peers // 2
    for n in range(2):
        part_rows = slice(n * part * slots, (n + 1) * part * slots)
        out = jnp.where(live[part_rows], dot(pick[part_rows], x_ref[...]), DEAD)
        out_ref[n * part : (n + 1) * part] = out.astype(BF16).reshape(part, slots, width)
        store = pltpu.make_async_copy(
            out_ref.at[pl.ds(n * part, part)], out_hbm.at[pl.ds(n * part, part)], sems.at[3 + n]
        )
        store.start()
        stores.append(store)
    for store in stores:
        store.wait()


def local_kernel(
    columns_ref,
    group_ref,
    values_ref,
    x_ref,
    weight_self_ref,
    target_ref,
    query_ref,
    positive_ref,
    negative_ref,
    local_ref,
    degree_ref,
    self_ref,
    pair_ref,
    target_hot_ref,
    negative_hot_ref,
    x_negative_ref,
    x_turned_ref,
):
    row_blocks, tiles_row, tile = values_ref.shape[1:4]
    nodes = x_ref.shape[0]
    peers, slots = target_ref.shape[1:]
    negatives = negative_ref.shape[1]
    queries = query_ref.shape[1]
    candidates = pair_ref.shape[1]

    relative = positive_ref[...] - group_ref[0] * negatives
    relative = jnp.where(relative < 0, relative + candidates, relative)
    query_hot = one_hot(iota((nodes, queries), 0) == query_ref[...])
    positive_hot = one_hot(iota((candidates, queries), 0) == relative)
    pair_ref[...] = dot(query_hot, positive_hot, 1, 1)

    square = (negatives, negatives)
    negative = jnp.sum(
        jnp.where(iota(square, 0) == iota(square, 1), negative_ref[...].astype(F32), 0.0),
        axis=1,
        keepdims=True,
    )
    negative_hot = one_hot(iota((negatives, nodes), 1).astype(F32) == negative)
    negative_hot_ref[...] = negative_hot
    x_negative_ref[...] = dot(negative_hot, x_ref[...]).astype(BF16)

    ones = jnp.ones((tile, 128), BF16)
    for block in range(row_blocks):
        total = jnp.zeros((tile, x_ref.shape[1]), F32)
        weight = jnp.ones((tile, 128), F32)
        for t in range(tiles_row):
            first = pl.multiple_of(columns_ref[0, block, t] * tile, tile)
            values = values_ref[0, block, t]
            total += dot(values, x_ref[pl.ds(first, tile), :])
            weight += dot(values, ones)
        local_ref[block * tile : (block + 1) * tile, :] = total
        degree_ref[block * tile : (block + 1) * tile, :] = weight

    self_ref[...] = dot(x_ref[...], weight_self_ref[...])
    x_turned_ref[...] = x_ref[...].T.reshape(x_turned_ref.shape)

    total = peers * slots
    shape = (peers, total)
    column, first = iota(shape, 1), iota(shape, 0) * slots
    mine = (column >= first) & (column < first + slots)
    start = jnp.sum(jnp.where(mine, first.astype(F32), 0.0), axis=0, keepdims=True)
    place = iota((1, total), 1).astype(F32) - start
    spread = one_hot(iota((slots, total), 0).astype(F32) == place)
    table = dot(target_ref[0].astype(F32).astype(BF16), spread)
    target = jnp.sum(jnp.where(mine, table, 0.0), axis=0, keepdims=True)
    target_hot_ref[...] = one_hot(iota((nodes, total), 0).astype(F32) == target)


def aggregate_kernel(
    received_ref,
    target_hot_ref,
    local_ref,
    degree_ref,
    negative_hot_ref,
    out_ref,
    negative_ref,
):
    received = received_ref[...].astype(F32)
    live = received[:, :1] < DEAD_FLOOR
    weighted = jnp.where(live, received, 0.0).astype(BF16)
    flags = jnp.broadcast_to(jnp.where(live, 1.0, 0.0), (received.shape[0], 128)).astype(BF16)
    hot = target_hot_ref[...]
    degree = degree_ref[...] + dot(hot, flags)
    summed = local_ref[...] + dot(hot, weighted)
    width = summed.shape[1]
    for first in range(0, width, 128):
        out_ref[:, first : first + 128] = (summed[:, first : first + 128] / degree).astype(BF16)
    negative_ref[...] = dot(negative_hot_ref[...], out_ref[...]).astype(BF16)


def embed_kernel(
    self_ref,
    aggregate_ref,
    weight_neigh_ref,
    embeds_hbm,
    embeds_ref,
    exact_ref,
    scale_ref,
    turned_ref,
    sem,
):
    aggregate = aggregate_ref[...]
    pre = self_ref[...] + dot(aggregate, weight_neigh_ref[...])
    scale = lax.rsqrt(jnp.mean(pre * pre, axis=1, keepdims=True) + EPSILON)
    exact = pre * scale
    embeds_ref[...] = exact.astype(BF16)
    copy = pltpu.make_async_copy(embeds_ref, embeds_hbm, sem)
    copy.start()
    exact_ref[...] = exact
    scale_ref[...] = jnp.broadcast_to(scale, scale_ref.shape)
    turned_ref[...] = aggregate.T.reshape(turned_ref.shape)
    copy.wait()


def split_dot(left, right, left_axis):
    high = left.astype(BF16)
    low = (left - high.astype(F32)).astype(BF16)
    return dot(high, right, left_axis, 0) + dot(low, right, left_axis, 0)


def gradient_kernel(
    query_total,
    core_ref,
    x_cand_ref,
    aggregate_cand_ref,
    weight_self_ref,
    weight_neigh_ref,
    embeds_ref,
    exact_ref,
    scale_ref,
    pair_ref,
    x_turned_ref,
    aggregate_turned_ref,
    keep_ref,
    send_ref,
    x_cand_turned_ref,
    aggregate_cand_turned_ref,
):
    width = embeds_ref.shape[1]
    score_factor = 1.0 / math.sqrt(width)
    candidates = x_cand_ref.shape[0]

    x_cand, aggregate_cand = x_cand_ref[...], aggregate_cand_ref[...]
    pre = dot(x_cand, weight_self_ref[...]) + dot(aggregate_cand, weight_neigh_ref[...])
    scale_cand = lax.rsqrt(jnp.mean(pre * pre, axis=1, keepdims=True) + EPSILON)
    exact_cand = pre * scale_cand
    cand = exact_cand.astype(BF16)

    embeds = embeds_ref[...]
    scores = score_factor * dot(embeds, cand, 1, 1)
    sigma = jax.nn.sigmoid(scores)
    factor = LOSS_FACTOR / query_total
    at_positive = ((sigma - 1.0) * factor).astype(BF16).astype(F32)
    elsewhere = ((sigma / (candidates - 1.0)) * factor).astype(BF16).astype(F32)
    pair = pair_ref[...]
    count = jnp.sum(pair, axis=1, keepdims=True)
    grad = (count - pair) * elsewhere + pair * at_positive

    emb_grad = score_factor * split_dot(grad, cand, 1)
    cand_grad = score_factor * split_dot(grad, embeds, 0)

    def through_norm(given, exact, scale):
        inner = jnp.mean(exact * given, axis=1, keepdims=True)
        return (scale * (given - exact * inner)).astype(BF16)

    pre_grad = through_norm(emb_grad, exact_ref[...], scale_ref[:, :1])
    pre_grad_cand = through_norm(cand_grad, exact_cand, scale_cand)

    half, _, rows, _ = x_turned_ref.shape
    x_cand_turned_ref[...] = x_cand.T.reshape(half, 2, rows, candidates)
    aggregate_cand_turned_ref[...] = aggregate_cand.T.reshape(half, 2, rows, candidates)
    own = core_ref[0]
    parts = (
        (x_turned_ref, x_cand_turned_ref),
        (aggregate_turned_ref, aggregate_cand_turned_ref),
    )
    for ref, core in ((send_ref, 1 - own), (keep_ref, own)):
        for part, (turned_ref, cand_turned_ref) in enumerate(parts):
            left = turned_ref[:, core].reshape(half * rows, turned_ref.shape[3])
            left_cand = cand_turned_ref[:, core].reshape(half * rows, candidates)
            block = dot(left, pre_grad) + dot(left_cand, pre_grad_cand)
            ref[part * half : (part + 1) * half] = block.reshape(half, rows, width).astype(BF16)


VMEM = pl.BlockSpec(memory_space=pltpu.VMEM)
SMEM = pl.BlockSpec(memory_space=pltpu.SMEM)
HBM = pl.BlockSpec(memory_space=pltpu.HBM)


def call(kernel, name, outs, args, flops=0, scratch=(), grant=16 << 20):
    shapes = [jax.ShapeDtypeStruct(shape, kind) for shape, kind, _ in outs]
    arrays = [a for a, _ in args]
    moved = sum(math.prod(a.shape) * a.dtype.itemsize for a in arrays + shapes)
    return pl.pallas_call(
        kernel,
        name=name,
        out_shape=shapes,
        in_specs=[place for _, place in args],
        out_specs=[place for _, _, place in outs],
        scratch_shapes=list(scratch),
        compiler_params=pltpu.CompilerParams(vmem_limit_bytes=grant),
        cost_estimate=pl.CostEstimate(flops=flops, bytes_accessed=moved, transcendentals=0),
    )(*arrays)


def on_device(
    features,
    tile_columns,
    tile_values,
    send_rows,
    send_count,
    ghost_target,
    query_rows,
    positive_cand,
    negative_rows,
    weight_self,
    weight_neigh,
):
    nodes, width = features.shape
    peers, slots = send_rows.shape[1:]
    total = peers * slots
    negatives = negative_rows.shape[1]
    groups = lax.axis_size("group")
    candidates = negatives * groups
    chips = peers // 2
    rows = 2 * width // peers
    half = chips // 2
    group = lax.axis_index("group").astype(jnp.int32)
    core = (lax.axis_index("dom") & 1).astype(jnp.int32)

    (outgoing,) = call(
        pack_kernel,
        "pack",
        [((peers, slots, width), BF16, HBM)],
        [(send_rows, HBM), (send_count, HBM), (features, HBM)],
        flops=2 * total * nodes * width,
        scratch=[
            pltpu.VMEM(send_rows.shape, jnp.int32),
            pltpu.VMEM(send_count.shape, jnp.int32),
            pltpu.VMEM(features.shape, BF16),
            pltpu.VMEM((peers, slots, width), BF16),
            pltpu.SemaphoreType.DMA((5,)),
        ],
        grant=None,
    )
    received = lax.all_to_all(
        outgoing, "dom", split_axis=0, concat_axis=0, tiled=True
    ).reshape(total, width)
    local, degree, own_pre, pair, target_hot, negative_hot, x_negative, x_turned = call(
        local_kernel,
        "local",
        [
            ((nodes, width), F32, VMEM),
            ((nodes, 128), F32, VMEM),
            ((nodes, width), F32, VMEM),
            ((nodes, candidates), F32, VMEM),
            ((nodes, total), BF16, VMEM),
            ((negatives, nodes), BF16, VMEM),
            ((negatives, width), BF16, VMEM),
            ((half, 2, rows, nodes), BF16, VMEM),
        ],
        [
            (tile_columns, SMEM),
            (group.reshape(1), SMEM),
            (tile_values, VMEM),
            (features, VMEM),
            (weight_self, VMEM),
            (ghost_target, VMEM),
            (query_rows, VMEM),
            (positive_cand, VMEM),
            (negative_rows, VMEM),
        ],
        flops=2 * nodes * width * (width + tile_values.shape[2] * tile_values.shape[3]),
    )

    def gathered(own):
        blocks = [own]
        for k in range(1, groups):
            pairs = [((g + k) % groups, g) for g in range(groups)]
            blocks.append(lax.ppermute(own, "group", pairs))
        return jnp.concatenate(blocks, axis=0)

    x_cand = gathered(x_negative)
    aggregate, aggregate_negative = call(
        aggregate_kernel,
        "aggregate",
        [((nodes, width), BF16, VMEM), ((negatives, width), BF16, VMEM)],
        [(a, VMEM) for a in (received, target_hot, local, degree, negative_hot)],
        flops=2 * nodes * total * width,
    )
    aggregate_cand = gathered(aggregate_negative)
    embeds_out, embeds, exact, scale, aggregate_turned = call(
        embed_kernel,
        "embed",
        [
            ((nodes, width), BF16, HBM),
            ((nodes, width), BF16, VMEM),
            ((nodes, width), F32, VMEM),
            ((nodes, 128), F32, VMEM),
            ((half, 2, rows, nodes), BF16, VMEM),
        ],
        [(own_pre, VMEM), (aggregate, VMEM), (weight_neigh, VMEM)],
        flops=2 * nodes * width * width,
        scratch=[pltpu.SemaphoreType.DMA],
    )
    keep, send = call(
        functools.partial(gradient_kernel, query_rows.shape[1]),
        "gradient",
        [((chips, rows, width), BF16, VMEM)] * 2,
        [(core.reshape(1), SMEM)]
        + [
            (a, VMEM)
            for a in (
                x_cand,
                aggregate_cand,
                weight_self,
                weight_neigh,
                embeds,
                exact,
                scale,
                pair,
                x_turned,
                aggregate_turned,
            )
        ],
        flops=4 * nodes * width * width,
        scratch=[pltpu.VMEM((half, 2, rows, candidates), BF16)] * 2,
    )

    swap = [(i, i ^ 1) for i in range(peers)]
    same_core = [[c + 2 * chip for chip in range(chips)] for c in range(2)]
    chip_sum = (keep.astype(F32) + lax.ppermute(send, "dom", swap).astype(F32)).astype(BF16)
    parts = lax.all_to_all(
        chip_sum,
        "dom",
        split_axis=0,
        concat_axis=0,
        axis_index_groups=same_core,
        tiled=True,
    )
    shard = jnp.sum(parts.astype(F32), axis=0).astype(BF16)
    if groups == 2:
        other = lax.ppermute(shard, "group", [(0, 1), (1, 0)])
        shard = (shard.astype(F32) + other.astype(F32)).astype(BF16)
    else:
        shard = lax.psum(shard, "group")
    return (embeds_out, shard)


def solution(mesh):
    placed = (
        P(("group", "dom"), None),
        P(("group", "dom"), None, None),
        P(("group", "dom"), None, None, None, None),
        P(("group", "dom"), None, None),
        P(("group", "dom"), None),
        P(("group", "dom"), None, None),
        P(("group", "dom"), None),
        P(("group", "dom"), None),
        P(("group", "dom"), None),
        P(),
        P(),
    )
    return jax.shard_map(
        on_device,
        mesh=mesh,
        in_specs=placed,
        out_specs=(P(("group", "dom"), None), P("dom", None)),
        check_vma=False,
    )
```

```python
import functools
import math

import jax
import jax.numpy as jnp
from jax import lax
from jax.experimental import pallas as pl
from jax.experimental.pallas import tpu as pltpu
from jax.sharding import PartitionSpec as P

LOSS_FACTOR = 64.0
EPSILON = 1e-05
DEAD = 256.0
DEAD_FLOOR = 128.0

F32 = jnp.float32
BF16 = jnp.bfloat16


def iota(shape, axis):
    return lax.broadcasted_iota(jnp.int32, shape, axis)


def dot(left, right, left_axis=1, right_axis=0):
    return lax.dot_general(
        left, right, (((left_axis,), (right_axis,)), ((), ())), preferred_element_type=F32
    )


def one_hot(condition):
    return jnp.where(condition, 1.0, 0.0).astype(BF16)


def pack_kernel(
    rows_hbm,
    count_hbm,
    x_hbm,
    query_hbm,
    positive_hbm,
    negative_hbm,
    out_hbm,
    joined_hbm,
    rows_ref,
    count_ref,
    x_ref,
    query_ref,
    positive_ref,
    negative_ref,
    out_ref,
    wide_ref,
    ids_ref,
    sems,
):
    places = (
        (rows_hbm, rows_ref),
        (count_hbm, count_ref),
        (x_hbm, x_ref),
        (query_hbm, query_ref),
        (positive_hbm, positive_ref),
        (negative_hbm, negative_ref),
    )
    loads = [pltpu.make_async_copy(*pair, sems.at[n]) for n, pair in enumerate(places)]
    for load in loads:
        load.start()
    peers, slots = rows_ref.shape[1:]
    nodes, width = x_ref.shape
    total = peers * slots
    row, first = iota((total, peers), 0), iota((total, peers), 1) * slots
    mine = (row >= first) & (row < first + slots)
    start = jnp.sum(jnp.where(mine, first.astype(F32), 0.0), axis=1, keepdims=True)
    place = row[:, :1].astype(F32) - start
    at_place = iota((total, slots), 1).astype(F32) == place
    peer = one_hot(mine)
    loads[0].wait()
    loads[1].wait()
    table = dot(peer, rows_ref[0].astype(F32).astype(BF16))
    index = jnp.sum(jnp.where(at_place, table, 0.0), axis=1, keepdims=True)
    count = jnp.sum(jnp.where(mine, count_ref[...].astype(F32), 0.0), axis=1, keepdims=True)
    live = place < count
    pick = one_hot(iota((total, nodes), 1).astype(F32) == index)
    loads[2].wait()
    stores = [pltpu.make_async_copy(x_ref, joined_hbm.at[pl.ds(0, nodes)], sems.at[len(loads)])]
    part = peers // 4
    for n in range(4):
        part_rows = slice(n * part * slots, (n + 1) * part * slots)
        out = jnp.where(live[part_rows], dot(pick[part_rows], x_ref[...]), DEAD)
        out_ref[n * part : (n + 1) * part] = out.astype(BF16).reshape(part, slots, width)
        piece = pl.ds(n * part, part)
        stores.append(
            pltpu.make_async_copy(out_ref.at[piece], out_hbm.at[piece], sems.at[len(loads) + 1 + n])
        )
        stores[-1].start()
    stores[0].start()
    for load in loads[3:]:
        load.wait()
    wide_ref[...] = jnp.zeros_like(wide_ref)
    for n, ref in enumerate((query_ref, positive_ref, negative_ref)):
        wide_ref[n : n + 1, : ref.shape[1]] = ref[...].astype(F32)
    ids_ref[...] = wide_ref[...].astype(BF16)
    ids = pltpu.make_async_copy(
        ids_ref, joined_hbm.at[pl.ds(nodes, ids_ref.shape[0])], sems.at[len(loads) + 5]
    )
    ids.start()
    for store in stores + [ids]:
        store.wait()


def local_kernel(columns_ref, values_ref, x_ref, target_ref, local_ref, degree_ref):
    row_blocks, tiles_row, tile = values_ref.shape[1:4]
    nodes = x_ref.shape[0]
    peers, slots = target_ref.shape[1:]

    ones = jnp.ones((tile, 128), BF16)
    for block in range(row_blocks):
        total = jnp.zeros((tile, x_ref.shape[1]), F32)
        weight = jnp.ones((tile, 128), F32)
        for t in range(tiles_row):
            first = pl.multiple_of(columns_ref[0, block, t] * tile, tile)
            values = values_ref[0, block, t]
            total += dot(values, x_ref[pl.ds(first, tile), :])
            weight += dot(values, ones)
        local_ref[block * tile : (block + 1) * tile, :] = total
        degree_ref[block * tile : (block + 1) * tile, :128] = weight

    total = peers * slots
    shape = (peers, total)
    column, first = iota(shape, 1), iota(shape, 0) * slots
    mine = (column >= first) & (column < first + slots)
    start = jnp.sum(jnp.where(mine, first.astype(F32), 0.0), axis=0, keepdims=True)
    place = iota((1, total), 1).astype(F32) - start
    spread = one_hot(iota((slots, total), 0).astype(F32) == place)
    table = dot(target_ref[0].astype(F32).astype(BF16), spread)
    target = jnp.sum(jnp.where(mine, table, 0.0), axis=0, keepdims=True)
    degree_ref[:, 128:] = jnp.where(iota((nodes, total), 0).astype(F32) == target, 1.0, 0.0)


def aggregate_kernel(received_ref, local_ref, degree_ref, out_ref):
    received = received_ref[...].astype(F32)
    live = received[:, :1] < DEAD_FLOOR
    weighted = jnp.where(live, received, 0.0).astype(BF16)
    flags = jnp.broadcast_to(jnp.where(live, 1.0, 0.0), (received.shape[0], 128)).astype(BF16)
    hot = degree_ref[:, 128:].astype(BF16)
    degree = degree_ref[:, :128] + dot(hot, flags)
    summed = local_ref[...] + dot(hot, weighted)
    width = summed.shape[1]
    for first in range(0, width, 128):
        out_ref[:, first : first + 128] = (summed[:, first : first + 128] / degree).astype(BF16)


def normed(pre):
    scale = lax.rsqrt(jnp.mean(pre * pre, axis=1, keepdims=True) + EPSILON)
    return pre * scale, scale


def columns_of(group, members, whole):
    columns = whole.shape[1] // members
    part = whole[:, :columns]
    for other in range(1, members):
        there = whole[:, other * columns : (other + 1) * columns]
        part = jnp.where(group == other, there, part)
    return part


def embed_kernel(
    members,
    sizes,
    group_ref,
    aggregate_ref,
    weight_self_ref,
    weight_neigh_ref,
    *refs,
):
    queries, negatives = sizes
    candidates = members * negatives
    joined, refs = refs[:members], refs[members:]
    (embeds_hbm, embeds_ref, part_ref, scale_ref, turned_ref), refs = refs[:5], refs[5:]
    (pair_ref, rest_ref, hot_ref, hot_turned_ref), refs = refs[:4], refs[4:]
    pres, x_turned, sem = refs[: members - 1], refs[members - 1 : -1], refs[-1]
    aggregate = aggregate_ref[...]
    nodes = aggregate.shape[0]

    own_pre = dot(joined[0][:nodes], weight_self_ref[...])
    exact, scale = normed(own_pre + dot(aggregate, weight_neigh_ref[...]))
    embeds_ref[...] = exact.astype(BF16)
    copy = pltpu.make_async_copy(embeds_ref, embeds_hbm, sem)
    copy.start()
    part_ref[...] = columns_of(group_ref[0], members, exact)
    scale_ref[...] = jnp.broadcast_to(scale, scale_ref.shape)
    turned_ref[...] = aggregate.T.reshape(turned_ref.shape)

    for member, joined_ref in enumerate(joined):
        if member:
            pres[member - 1][...] = dot(joined_ref[:nodes], weight_self_ref[...])
        x_turned[member][...] = joined_ref[:nodes].T.reshape(x_turned[member].shape)
        ids = joined_ref[nodes:].astype(F32)
        query, negative = ids[:1, :queries], ids[2:3, :negatives]
        relative = ids[1:2, :queries] - (group_ref[0] * negatives).astype(F32)
        relative = jnp.where(relative < 0.0, relative + candidates, relative)
        query_hot = one_hot(iota((nodes, queries), 0).astype(F32) == query)
        positive_hot = one_hot(iota((candidates, queries), 0).astype(F32) == relative)
        pair = dot(query_hot, positive_hot, 1, 1)
        lanes = slice(member * candidates, (member + 1) * candidates)
        pair_ref[:, lanes] = pair
        rest_ref[:, lanes] = jnp.sum(pair, axis=1, keepdims=True) - pair
        square = (negatives, negatives)
        column = jnp.where(iota(square, 0) == iota(square, 1), negative, 0.0)
        column = jnp.sum(column, axis=1, keepdims=True)
        hot_ref[member] = one_hot(iota((negatives, nodes), 1).astype(F32) == column)
        turned = one_hot(iota((nodes, negatives), 0).astype(F32) == negative)
        hot_turned_ref[:, member * negatives : (member + 1) * negatives] = turned
    copy.wait()


def rows_of_core(core, ref, lefts, rights):
    half, _, rows, nodes = lefts[0][0].shape
    columns = ref.shape[2]
    for part, left_refs in enumerate(lefts):
        block = jnp.zeros((half * rows, columns), F32)
        for left_ref, right in zip(left_refs, rights):
            block += dot(left_ref[:, core].reshape(half * rows, nodes), right)
        ref[part * half : (part + 1) * half] = block.reshape(half, rows, columns).astype(BF16)


def keep_kernel(core_ref, *refs):
    *refs, keep_ref = refs
    members = len(refs) // 3
    lefts = (refs[:members], refs[members : 2 * members])
    rows_of_core(core_ref[0], keep_ref, lefts, [ref[...] for ref in refs[2 * members :]])


def gradient_kernel(
    query_total,
    core_ref,
    group_ref,
    weight_neigh_ref,
    embeds_ref,
    part_ref,
    scale_ref,
    pair_ref,
    rest_ref,
    hot_ref,
    hot_turned_ref,
    x_turned_ref,
    turned_ref,
    *refs,
):
    members, negatives, _ = hot_ref.shape
    others = members - 1
    given, refs = refs[: 3 * others], refs[3 * others :]
    send_ref, pre_grad_refs, other_turned = refs[0], refs[1 : 1 + members], refs[1 + members :]
    candidates = members * negatives
    width = embeds_ref.shape[1]
    columns = width // members
    group = group_ref[0]
    score_factor = 1.0 / math.sqrt(width)
    factor = LOSS_FACTOR / query_total

    parts, scales, embeds = [part_ref[...]], [scale_ref[:, :1]], [embeds_ref[...]]
    x_turned, turned = [x_turned_ref], [turned_ref]
    for other, other_turned_ref in enumerate(other_turned):
        aggregate_ref, pre_ref, other_x_turned_ref = given[3 * other : 3 * other + 3]
        aggregate = aggregate_ref[...]
        exact, scale = normed(pre_ref[...] + dot(aggregate, weight_neigh_ref[...]))
        parts.append(columns_of(group, members, exact))
        scales.append(scale)
        embeds.append(exact.astype(BF16))
        other_turned_ref[...] = aggregate.T.reshape(other_turned_ref.shape)
        x_turned.append(other_x_turned_ref)
        turned.append(other_turned_ref)

    cand = jnp.concatenate(
        [dot(hot_ref[m], embeds[m]).astype(BF16) for m in range(members)], axis=0
    )

    def at(member, block, count=members):
        zero = jnp.zeros_like(block)
        return jnp.concatenate([block if n == member else zero for n in range(count)], axis=0)

    product = sum(dot(embeds[m], at(m, cand), 1, 1) for m in range(members))
    sigma = jax.nn.sigmoid(score_factor * product)
    at_positive = ((sigma - 1.0) * factor).astype(BF16).astype(F32)
    elsewhere = ((sigma / (candidates - 1.0)) * factor).astype(BF16).astype(F32)
    grad = score_factor * (rest_ref[...] * elsewhere + pair_ref[...] * at_positive)
    grad = grad.astype(BF16)

    weighted = grad.astype(F32) * product
    as_cand = jnp.sum(weighted, axis=0, keepdims=True)
    as_cand = sum(as_cand[:, m * candidates : (m + 1) * candidates] for m in range(members))
    hot_turned = hot_turned_ref[...]
    as_cand = hot_turned.astype(F32) * as_cand

    cand_part = columns_of(group, members, cand)
    cand_grad = sum(
        dot(grad, parts[m].astype(BF16), 0, 0)[m * candidates : (m + 1) * candidates]
        for m in range(members)
    ).astype(BF16)
    left = jnp.concatenate([grad, hot_turned], axis=1)
    pre_grads = []
    for m in range(members):
        mine = slice(m * negatives, (m + 1) * negatives)
        right = jnp.concatenate([at(m, cand_part), at(m, cand_grad[mine])], axis=0)
        inner = jnp.sum(
            weighted[:, m * candidates : (m + 1) * candidates], axis=1, keepdims=True
        ) + jnp.sum(as_cand[:, mine], axis=1, keepdims=True)
        pre_grad = scales[m] * (dot(left, right) - parts[m] * (inner / width))
        pre_grads.append(pre_grad.astype(BF16))

    for ref, pre_grad in zip(pre_grad_refs, pre_grads):
        ref[...] = pre_grad
    rows_of_core(1 - core_ref[0], send_ref, (x_turned, turned), pre_grads)


VMEM = pl.BlockSpec(memory_space=pltpu.VMEM)
SMEM = pl.BlockSpec(memory_space=pltpu.SMEM)
HBM = pl.BlockSpec(memory_space=pltpu.HBM)


def call(kernel, name, outs, args, flops=0, scratch=(), grant=16 << 20):
    shapes = [jax.ShapeDtypeStruct(shape, kind) for shape, kind, _ in outs]
    arrays = [a for a, _ in args]
    moved = sum(math.prod(a.shape) * a.dtype.itemsize for a in arrays + shapes)
    return pl.pallas_call(
        kernel,
        name=name,
        out_shape=shapes,
        in_specs=[place for _, place in args],
        out_specs=[place for _, _, place in outs],
        scratch_shapes=list(scratch),
        compiler_params=pltpu.CompilerParams(vmem_limit_bytes=grant),
        cost_estimate=pl.CostEstimate(flops=flops, bytes_accessed=moved, transcendentals=0),
    )(*arrays)


def on_device(
    features,
    tile_columns,
    tile_values,
    send_rows,
    send_count,
    ghost_target,
    query_rows,
    positive_cand,
    negative_rows,
    weight_self,
    weight_neigh,
):
    nodes, width = features.shape
    peers, slots = send_rows.shape[1:]
    total = peers * slots
    queries = query_rows.shape[1]
    negatives = negative_rows.shape[1]
    groups = lax.axis_size("group")
    others = groups - 1
    candidates = negatives * groups
    chips = peers // 2
    rows = 2 * width // peers
    half = chips // 2
    columns = width // groups
    grant = min(8 * groups, 56) << 20
    group = lax.axis_index("group").astype(jnp.int32)
    core = (lax.axis_index("dom") & 1).astype(jnp.int32)

    def of_others(own):
        return [
            lax.ppermute(own, "group", [((g + k) % groups, g) for g in range(groups)])
            for k in range(1, groups)
        ]

    id_rows = 16
    outgoing, joined = call(
        pack_kernel,
        "pack",
        [((peers, slots, width), BF16, HBM), ((nodes + id_rows, width), BF16, HBM)],
        [
            (a, HBM)
            for a in (
                send_rows, send_count, features, query_rows, positive_cand, negative_rows
            )
        ],
        flops=2 * total * nodes * width,
        scratch=[
            pltpu.VMEM(send_rows.shape, jnp.int32),
            pltpu.VMEM(send_count.shape, jnp.int32),
            pltpu.VMEM(features.shape, BF16),
            pltpu.VMEM(query_rows.shape, jnp.int32),
            pltpu.VMEM(positive_cand.shape, jnp.int32),
            pltpu.VMEM(negative_rows.shape, jnp.int32),
            pltpu.VMEM((peers, slots, width), BF16),
            pltpu.VMEM((id_rows, width), F32),
            pltpu.VMEM((id_rows, width), BF16),
            pltpu.SemaphoreType.DMA((12,)),
        ],
        grant=None,
    )
    received = lax.all_to_all(
        outgoing, "dom", split_axis=0, concat_axis=0, tiled=True
    ).reshape(total, width)

    joined = [joined] + of_others(joined)
    local, degree = call(
        local_kernel,
        "local",
        [((nodes, width), F32, VMEM), ((nodes, 128 + total), F32, VMEM)],
        [(tile_columns, SMEM), (tile_values, VMEM), (features, VMEM), (ghost_target, VMEM)],
        flops=2 * nodes * width * tile_values.shape[2] * tile_values.shape[3],
        grant=grant,
    )
    (aggregate,) = call(
        aggregate_kernel,
        "aggregate",
        [((nodes, width), BF16, VMEM)],
        [(a, VMEM) for a in (received, local, degree)],
        flops=2 * nodes * total * width,
    )
    other_aggregate = of_others(aggregate)
    node_turned = ((half, 2, rows, nodes), BF16, VMEM)
    core, group_place = core.reshape(1), (group.reshape(1), SMEM)
    embeds_out, embeds, part, scale, turned, pair, rest, hot, hot_turned, *made = call(
        functools.partial(embed_kernel, groups, (queries, negatives)),
        "embed",
        [
            ((nodes, width), BF16, HBM),
            ((nodes, width), BF16, VMEM),
            ((nodes, columns), F32, VMEM),
            ((nodes, 128), F32, VMEM),
            node_turned,
            ((nodes, groups * candidates), F32, VMEM),
            ((nodes, groups * candidates), F32, VMEM),
            ((groups, negatives, nodes), BF16, VMEM),
            ((nodes, candidates), BF16, VMEM),
        ]
        + [((nodes, width), F32, VMEM)] * others
        + [node_turned] * groups,
        [group_place]
        + [(a, VMEM) for a in (aggregate, weight_self, weight_neigh, *joined)],
        flops=2 * nodes * width * width * groups,
        scratch=[pltpu.SemaphoreType.DMA],
        grant=grant,
    )
    x_turned, *features_turned = made[others:]
    members = []
    for trio in zip(other_aggregate, made[:others], features_turned):
        members += trio
    send, *made = call(
        functools.partial(gradient_kernel, queries),
        "gradient",
        [((chips, rows, columns), BF16, VMEM)]
        + [((nodes, columns), BF16, VMEM)] * groups
        + [node_turned] * others,
        [(core, SMEM), group_place]
        + [
            (a, VMEM)
            for a in (
                weight_neigh,
                embeds,
                part,
                scale,
                pair,
                rest,
                hot,
                hot_turned,
                x_turned,
                turned,
                *members,
            )
        ],
        flops=2 * nodes * width * width,
        grant=grant,
    )
    features_turned = [x_turned] + features_turned
    aggregates_turned = [turned] + made[groups:]
    (keep,) = call(
        keep_kernel,
        "keep",
        [((chips, rows, columns), BF16, VMEM)],
        [(core, SMEM)]
        + [(a, VMEM) for a in (*features_turned, *aggregates_turned, *made[:groups])],
        flops=2 * nodes * width * width,
        grant=grant,
    )

    swap = [(i, i ^ 1) for i in range(peers)]
    same_core = [[c + 2 * chip for chip in range(chips)] for c in range(2)]
    chip_sum = (keep.astype(F32) + lax.ppermute(send, "dom", swap).astype(F32)).astype(BF16)
    parts = lax.all_to_all(
        chip_sum,
        "dom",
        split_axis=0,
        concat_axis=0,
        axis_index_groups=same_core,
        tiled=True,
    )
    summed = jnp.sum(parts.astype(F32), axis=0).astype(BF16)
    if groups == 2:
        (other,) = of_others(summed)
        shard = jnp.where(
            group == 0,
            jnp.concatenate([summed, other], axis=1),
            jnp.concatenate([other, summed], axis=1),
        )
    else:
        shard = lax.all_gather(summed, "group", axis=1, tiled=True)
    return (embeds_out, shard)


def solution(mesh):
    placed = (
        P(("group", "dom"), None),
        P(("group", "dom"), None, None),
        P(("group", "dom"), None, None, None, None),
        P(("group", "dom"), None, None),
        P(("group", "dom"), None),
        P(("group", "dom"), None, None),
        P(("group", "dom"), None),
        P(("group", "dom"), None),
        P(("group", "dom"), None),
        P(),
        P(),
    )
    return jax.shard_map(
        on_device,
        mesh=mesh,
        in_specs=placed,
        out_specs=(P(("group", "dom"), None), P("dom", None)),
        check_vma=False,
    )
```

```python
import functools
import math

import jax
import jax.numpy as jnp
from jax import lax
from jax.experimental import pallas as pl
from jax.experimental.pallas import tpu as pltpu
from jax.sharding import PartitionSpec as P

LOSS_FACTOR = 64.0
EPSILON = 1e-05
DEAD = 256.0
DEAD_FLOOR = 128.0

F32 = jnp.float32
BF16 = jnp.bfloat16


def iota(shape, axis):
    return lax.broadcasted_iota(jnp.int32, shape, axis)


def dot(left, right, left_axis=1, right_axis=0):
    return lax.dot_general(
        left, right, (((left_axis,), (right_axis,)), ((), ())), preferred_element_type=F32
    )


def one_hot(condition):
    return jnp.where(condition, 1.0, 0.0).astype(BF16)


def pack_kernel(
    rows_hbm,
    count_hbm,
    x_hbm,
    query_hbm,
    positive_hbm,
    negative_hbm,
    out_hbm,
    joined_hbm,
    rows_ref,
    count_ref,
    x_ref,
    query_ref,
    positive_ref,
    negative_ref,
    out_ref,
    wide_ref,
    ids_ref,
    sems,
):
    places = (
        (rows_hbm, rows_ref),
        (count_hbm, count_ref),
        (x_hbm, x_ref),
        (query_hbm, query_ref),
        (positive_hbm, positive_ref),
        (negative_hbm, negative_ref),
    )
    loads = [pltpu.make_async_copy(*pair, sems.at[n]) for n, pair in enumerate(places)]
    for load in loads:
        load.start()
    peers, slots = rows_ref.shape[1:]
    nodes, width = x_ref.shape
    total = peers * slots
    row, first = iota((total, peers), 0), iota((total, peers), 1) * slots
    mine = (row >= first) & (row < first + slots)
    start = jnp.sum(jnp.where(mine, first.astype(F32), 0.0), axis=1, keepdims=True)
    place = row[:, :1].astype(F32) - start
    at_place = iota((total, slots), 1).astype(F32) == place
    peer = one_hot(mine)
    loads[0].wait()
    loads[1].wait()
    table = dot(peer, rows_ref[0].astype(F32).astype(BF16))
    index = jnp.sum(jnp.where(at_place, table, 0.0), axis=1, keepdims=True)
    count = jnp.sum(jnp.where(mine, count_ref[...].astype(F32), 0.0), axis=1, keepdims=True)
    live = place < count
    pick = one_hot(iota((total, nodes), 1).astype(F32) == index)
    for load in loads[3:]:
        load.wait()
    wide_ref[...] = jnp.zeros_like(wide_ref)
    for n, ref in enumerate((query_ref, positive_ref, negative_ref)):
        wide_ref[n : n + 1, : ref.shape[1]] = ref[...].astype(F32)
    ids_ref[...] = wide_ref[...].astype(BF16)
    ids_place = joined_hbm.at[pl.ds(nodes, ids_ref.shape[0])]
    loads[2].wait()
    stores = [
        pltpu.make_async_copy(ids_ref, ids_place, sems.at[len(loads)]),
        pltpu.make_async_copy(x_ref, joined_hbm.at[pl.ds(0, nodes)], sems.at[len(loads) + 1]),
    ]
    for store in stores:
        store.start()
    part = peers // 2
    for n in range(2):
        part_rows = slice(n * part * slots, (n + 1) * part * slots)
        out = jnp.where(live[part_rows], dot(pick[part_rows], x_ref[...]), DEAD)
        out_ref[n * part : (n + 1) * part] = out.astype(BF16).reshape(part, slots, width)
        piece = pl.ds(n * part, part)
        stores.append(
            pltpu.make_async_copy(out_ref.at[piece], out_hbm.at[piece], sems.at[len(loads) + 2 + n])
        )
        stores[-1].start()
    for store in stores:
        store.wait()


def local_kernel(columns_ref, values_ref, x_ref, target_ref, local_ref, degree_ref):
    row_blocks, tiles_row, tile = values_ref.shape[1:4]
    nodes = x_ref.shape[0]
    peers, slots = target_ref.shape[1:]

    ones = jnp.ones((tile, 128), BF16)
    for block in range(row_blocks):
        total = jnp.zeros((tile, x_ref.shape[1]), F32)
        weight = jnp.ones((tile, 128), F32)
        for t in range(tiles_row):
            first = pl.multiple_of(columns_ref[0, block, t] * tile, tile)
            values = values_ref[0, block, t]
            total += dot(values, x_ref[pl.ds(first, tile), :])
            weight += dot(values, ones)
        local_ref[block * tile : (block + 1) * tile, :] = total
        degree_ref[block * tile : (block + 1) * tile, :128] = weight

    total = peers * slots
    shape = (peers, total)
    column, first = iota(shape, 1), iota(shape, 0) * slots
    mine = (column >= first) & (column < first + slots)
    start = jnp.sum(jnp.where(mine, first.astype(F32), 0.0), axis=0, keepdims=True)
    place = iota((1, total), 1).astype(F32) - start
    spread = one_hot(iota((slots, total), 0).astype(F32) == place)
    table = dot(target_ref[0].astype(F32).astype(BF16), spread)
    target = jnp.sum(jnp.where(mine, table, 0.0), axis=0, keepdims=True)
    degree_ref[:, 128:] = jnp.where(iota((nodes, total), 0).astype(F32) == target, 1.0, 0.0)


def aggregate_kernel(received_ref, local_ref, degree_ref, out_ref):
    received = received_ref[...].astype(F32)
    live = received[:, :1] < DEAD_FLOOR
    weighted = jnp.where(live, received, 0.0).astype(BF16)
    flags = jnp.broadcast_to(jnp.where(live, 1.0, 0.0), (received.shape[0], 128)).astype(BF16)
    hot = degree_ref[:, 128:].astype(BF16)
    degree = degree_ref[:, :128] + dot(hot, flags)
    summed = local_ref[...] + dot(hot, weighted)
    width = summed.shape[1]
    for first in range(0, width, 128):
        out_ref[:, first : first + 128] = (summed[:, first : first + 128] / degree).astype(BF16)


def normed(pre):
    scale = lax.rsqrt(jnp.mean(pre * pre, axis=1, keepdims=True) + EPSILON)
    return pre * scale, scale


def columns_of(group, members, whole):
    columns = whole.shape[1] // members
    part = whole[:, :columns]
    for other in range(1, members):
        there = whole[:, other * columns : (other + 1) * columns]
        part = jnp.where(group == other, there, part)
    return part


def embed_kernel(
    members,
    sizes,
    group_ref,
    aggregate_ref,
    weight_self_ref,
    weight_neigh_ref,
    *refs,
):
    queries, negatives = sizes
    candidates = members * negatives
    joined, refs = refs[:members], refs[members:]
    (embeds_hbm, embeds_ref, part_ref, scale_ref, turned_ref), refs = refs[:5], refs[5:]
    (pair_ref, rest_ref, hot_ref, hot_turned_ref), refs = refs[:4], refs[4:]
    pres, x_turned, sem = refs[: members - 1], refs[members - 1 : -1], refs[-1]
    aggregate = aggregate_ref[...]
    nodes = aggregate.shape[0]

    own_pre = dot(joined[0][:nodes], weight_self_ref[...])
    exact, scale = normed(own_pre + dot(aggregate, weight_neigh_ref[...]))
    embeds_ref[...] = exact.astype(BF16)
    copy = pltpu.make_async_copy(embeds_ref, embeds_hbm, sem)
    copy.start()
    part_ref[...] = columns_of(group_ref[0], members, exact)
    scale_ref[...] = jnp.broadcast_to(scale, scale_ref.shape)
    turned_ref[...] = aggregate.T.reshape(turned_ref.shape)

    for member, joined_ref in enumerate(joined):
        if member:
            pres[member - 1][...] = dot(joined_ref[:nodes], weight_self_ref[...])
        x_turned[member][...] = joined_ref[:nodes].T.reshape(x_turned[member].shape)
        ids = joined_ref[nodes:].astype(F32)
        query, negative = ids[:1, :queries], ids[2:3, :negatives]
        relative = ids[1:2, :queries] - (group_ref[0] * negatives).astype(F32)
        relative = jnp.where(relative < 0.0, relative + candidates, relative)
        query_hot = one_hot(iota((nodes, queries), 0).astype(F32) == query)
        positive_hot = one_hot(iota((candidates, queries), 0).astype(F32) == relative)
        pair = dot(query_hot, positive_hot, 1, 1)
        lanes = slice(member * candidates, (member + 1) * candidates)
        pair_ref[:, lanes] = pair
        rest_ref[:, lanes] = jnp.sum(pair, axis=1, keepdims=True) - pair
        square = (negatives, negatives)
        column = jnp.where(iota(square, 0) == iota(square, 1), negative, 0.0)
        column = jnp.sum(column, axis=1, keepdims=True)
        hot_ref[member] = one_hot(iota((negatives, nodes), 1).astype(F32) == column)
        turned = one_hot(iota((nodes, negatives), 0).astype(F32) == negative)
        blank = jnp.zeros((nodes, negatives), BF16)
        hot_turned_ref[:, lanes] = jnp.concatenate(
            [turned if n == member else blank for n in range(members)], axis=1
        )
    copy.wait()


def rows_of_core(core, ref, lefts, rights):
    half, _, rows, nodes = lefts[0][0].shape
    columns = ref.shape[2]
    for part, left_refs in enumerate(lefts):
        block = jnp.zeros((half * rows, columns), F32)
        for left_ref, right in zip(left_refs, rights):
            block += dot(left_ref[:, core].reshape(half * rows, nodes), right)
        ref[part * half : (part + 1) * half] = block.reshape(half, rows, columns).astype(BF16)


def keep_kernel(core_ref, *refs):
    *refs, keep_ref = refs
    members = len(refs) // 3
    lefts = (refs[:members], refs[members : 2 * members])
    rows_of_core(core_ref[0], keep_ref, lefts, [ref[...] for ref in refs[2 * members :]])


def gradient_kernel(
    query_total,
    core_ref,
    group_ref,
    weight_neigh_ref,
    embeds_ref,
    part_ref,
    scale_ref,
    pair_ref,
    rest_ref,
    hot_ref,
    hot_turned_ref,
    x_turned_ref,
    turned_ref,
    *refs,
):
    members, negatives, _ = hot_ref.shape
    others = members - 1
    given, refs = refs[: 3 * others], refs[3 * others :]
    send_ref, pre_grad_refs, other_turned = refs[0], refs[1 : 1 + members], refs[1 + members :]
    candidates = members * negatives
    width = embeds_ref.shape[1]
    columns = width // members
    group = group_ref[0]
    score_factor = 1.0 / math.sqrt(width)
    factor = LOSS_FACTOR / query_total

    parts, scales, embeds = [part_ref[...]], [scale_ref[:, :1]], [embeds_ref[...]]
    x_turned, turned = [x_turned_ref], [turned_ref]
    for other, other_turned_ref in enumerate(other_turned):
        aggregate_ref, pre_ref, other_x_turned_ref = given[3 * other : 3 * other + 3]
        aggregate = aggregate_ref[...]
        exact, scale = normed(pre_ref[...] + dot(aggregate, weight_neigh_ref[...]))
        parts.append(columns_of(group, members, exact))
        scales.append(scale)
        embeds.append(exact.astype(BF16))
        other_turned_ref[...] = aggregate.T.reshape(other_turned_ref.shape)
        x_turned.append(other_x_turned_ref)
        turned.append(other_turned_ref)

    cand = jnp.concatenate(
        [dot(hot_ref[m], embeds[m]).astype(BF16) for m in range(members)], axis=0
    )

    def at(member, block, count=members):
        zero = jnp.zeros_like(block)
        return jnp.concatenate([block if n == member else zero for n in range(count)], axis=0)

    product = sum(dot(embeds[m], at(m, cand), 1, 1) for m in range(members))
    sigma = jax.nn.sigmoid(score_factor * product)
    at_positive = ((sigma - 1.0) * factor).astype(BF16).astype(F32)
    elsewhere = ((sigma / (candidates - 1.0)) * factor).astype(BF16).astype(F32)
    grad = score_factor * (rest_ref[...] * elsewhere + pair_ref[...] * at_positive)
    grad = grad.astype(BF16)

    weighted = grad.astype(F32) * product
    hot_turned = hot_turned_ref[...]
    as_cand = jnp.sum(weighted, axis=0, keepdims=True)
    as_cand = sum(as_cand[:, m * candidates : (m + 1) * candidates] for m in range(members))
    weighted += hot_turned.astype(F32) * jnp.concatenate([as_cand] * members, axis=1)

    cand_part = columns_of(group, members, cand)
    grad_turned = grad.T
    cand_grad = sum(
        dot(grad_turned[m * candidates : (m + 1) * candidates], parts[m].astype(BF16))
        for m in range(members)
    ).astype(BF16)
    left = jnp.concatenate([grad, hot_turned], axis=1)
    lane = iota(weighted.shape, 1)
    pre_grads = []
    for m in range(members):
        right = jnp.concatenate([at(m, cand_part), at(m, cand_grad)], axis=0)
        mine = (lane >= m * candidates) & (lane < (m + 1) * candidates)
        inner = jnp.sum(jnp.where(mine, weighted, 0.0), axis=1, keepdims=True)
        pre_grad = scales[m] * (dot(left, right) - parts[m] * (inner / width))
        pre_grads.append(pre_grad.astype(BF16))

    for ref, pre_grad in zip(pre_grad_refs, pre_grads):
        ref[...] = pre_grad
    rows_of_core(1 - core_ref[0], send_ref, (x_turned, turned), pre_grads)


VMEM = pl.BlockSpec(memory_space=pltpu.VMEM)
SMEM = pl.BlockSpec(memory_space=pltpu.SMEM)
HBM = pl.BlockSpec(memory_space=pltpu.HBM)


def call(kernel, name, outs, args, flops=0, scratch=(), grant=16 << 20):
    shapes = [jax.ShapeDtypeStruct(shape, kind) for shape, kind, _ in outs]
    arrays = [a for a, _ in args]
    moved = sum(math.prod(a.shape) * a.dtype.itemsize for a in arrays + shapes)
    return pl.pallas_call(
        kernel,
        name=name,
        out_shape=shapes,
        in_specs=[place for _, place in args],
        out_specs=[place for _, _, place in outs],
        scratch_shapes=list(scratch),
        compiler_params=pltpu.CompilerParams(vmem_limit_bytes=grant),
        cost_estimate=pl.CostEstimate(flops=flops, bytes_accessed=moved, transcendentals=0),
    )(*arrays)


def on_device(
    features,
    tile_columns,
    tile_values,
    send_rows,
    send_count,
    ghost_target,
    query_rows,
    positive_cand,
    negative_rows,
    weight_self,
    weight_neigh,
):
    nodes, width = features.shape
    peers, slots = send_rows.shape[1:]
    total = peers * slots
    queries = query_rows.shape[1]
    negatives = negative_rows.shape[1]
    groups = lax.axis_size("group")
    others = groups - 1
    candidates = negatives * groups
    chips = peers // 2
    rows = 2 * width // peers
    half = chips // 2
    columns = width // groups
    grant = min(8 * groups, 56) << 20
    group = lax.axis_index("group").astype(jnp.int32)
    core = (lax.axis_index("dom") & 1).astype(jnp.int32)

    def of_others(own):
        return [
            lax.ppermute(own, "group", [((g + k) % groups, g) for g in range(groups)])
            for k in range(1, groups)
        ]

    id_rows = 16
    outgoing, joined = call(
        pack_kernel,
        "pack",
        [((peers, slots, width), BF16, HBM), ((nodes + id_rows, width), BF16, HBM)],
        [
            (a, HBM)
            for a in (
                send_rows, send_count, features, query_rows, positive_cand, negative_rows
            )
        ],
        flops=2 * total * nodes * width,
        scratch=[
            pltpu.VMEM(send_rows.shape, jnp.int32),
            pltpu.VMEM(send_count.shape, jnp.int32),
            pltpu.VMEM(features.shape, BF16),
            pltpu.VMEM(query_rows.shape, jnp.int32),
            pltpu.VMEM(positive_cand.shape, jnp.int32),
            pltpu.VMEM(negative_rows.shape, jnp.int32),
            pltpu.VMEM((peers, slots, width), BF16),
            pltpu.VMEM((id_rows, width), F32),
            pltpu.VMEM((id_rows, width), BF16),
            pltpu.SemaphoreType.DMA((10,)),
        ],
        grant=None,
    )
    received = lax.all_to_all(
        outgoing, "dom", split_axis=0, concat_axis=0, tiled=True
    ).reshape(total, width)

    joined = [joined] + of_others(joined)
    local, degree = call(
        local_kernel,
        "local",
        [((nodes, width), F32, VMEM), ((nodes, 128 + total), F32, VMEM)],
        [(tile_columns, SMEM), (tile_values, VMEM), (features, VMEM), (ghost_target, VMEM)],
        flops=2 * nodes * width * tile_values.shape[2] * tile_values.shape[3],
        grant=grant,
    )
    (aggregate,) = call(
        aggregate_kernel,
        "aggregate",
        [((nodes, width), BF16, VMEM)],
        [(a, VMEM) for a in (received, local, degree)],
        flops=2 * nodes * total * width,
    )
    other_aggregate = of_others(aggregate)
    node_turned = ((half, 2, rows, nodes), BF16, VMEM)
    core, group_place = core.reshape(1), (group.reshape(1), SMEM)
    embeds_out, embeds, part, scale, turned, pair, rest, hot, hot_turned, *made = call(
        functools.partial(embed_kernel, groups, (queries, negatives)),
        "embed",
        [
            ((nodes, width), BF16, HBM),
            ((nodes, width), BF16, VMEM),
            ((nodes, columns), F32, VMEM),
            ((nodes, 128), F32, VMEM),
            node_turned,
            ((nodes, groups * candidates), F32, VMEM),
            ((nodes, groups * candidates), F32, VMEM),
            ((groups, negatives, nodes), BF16, VMEM),
            ((nodes, groups * candidates), BF16, VMEM),
        ]
        + [((nodes, width), F32, VMEM)] * others
        + [node_turned] * groups,
        [group_place]
        + [(a, VMEM) for a in (aggregate, weight_self, weight_neigh, *joined)],
        flops=2 * nodes * width * width * groups,
        scratch=[pltpu.SemaphoreType.DMA],
        grant=grant,
    )
    x_turned, *features_turned = made[others:]
    members = []
    for trio in zip(other_aggregate, made[:others], features_turned):
        members += trio
    send, *made = call(
        functools.partial(gradient_kernel, queries),
        "gradient",
        [((chips, rows, columns), BF16, VMEM)]
        + [((nodes, columns), BF16, VMEM)] * groups
        + [node_turned] * others,
        [(core, SMEM), group_place]
        + [
            (a, VMEM)
            for a in (
                weight_neigh,
                embeds,
                part,
                scale,
                pair,
                rest,
                hot,
                hot_turned,
                x_turned,
                turned,
                *members,
            )
        ],
        flops=2 * nodes * width * width,
        grant=grant,
    )
    features_turned = [x_turned] + features_turned
    aggregates_turned = [turned] + made[groups:]
    (keep,) = call(
        keep_kernel,
        "keep",
        [((chips, rows, columns), BF16, VMEM)],
        [(core, SMEM)]
        + [(a, VMEM) for a in (*features_turned, *aggregates_turned, *made[:groups])],
        flops=2 * nodes * width * width,
        grant=grant,
    )

    swap = [(i, i ^ 1) for i in range(peers)]
    same_core = [[c + 2 * chip for chip in range(chips)] for c in range(2)]
    chip_sum = (keep.astype(F32) + lax.ppermute(send, "dom", swap).astype(F32)).astype(BF16)
    parts = lax.all_to_all(
        chip_sum,
        "dom",
        split_axis=0,
        concat_axis=0,
        axis_index_groups=same_core,
        tiled=True,
    )
    summed = jnp.sum(parts.astype(F32), axis=0).astype(BF16)
    if groups == 2:
        (other,) = of_others(summed)
        shard = jnp.where(
            group == 0,
            jnp.concatenate([summed, other], axis=1),
            jnp.concatenate([other, summed], axis=1),
        )
    else:
        shard = lax.all_gather(summed, "group", axis=1, tiled=True)
    return (embeds_out, shard)


def solution(mesh):
    placed = (
        P(("group", "dom"), None),
        P(("group", "dom"), None, None),
        P(("group", "dom"), None, None, None, None),
        P(("group", "dom"), None, None),
        P(("group", "dom"), None),
        P(("group", "dom"), None, None),
        P(("group", "dom"), None),
        P(("group", "dom"), None),
        P(("group", "dom"), None),
        P(),
        P(),
    )
    return jax.shard_map(
        on_device,
        mesh=mesh,
        in_specs=placed,
        out_specs=(P(("group", "dom"), None), P("dom", None)),
        check_vma=False,
    )
```

```python
import functools
import math

import jax
import jax.numpy as jnp
from jax import lax
from jax.experimental import pallas as pl
from jax.experimental.pallas import tpu as pltpu
from jax.sharding import PartitionSpec as P

LOSS_FACTOR = 64.0
EPSILON = 1e-05
DEAD = 256.0
DEAD_FLOOR = 128.0

F32 = jnp.float32
BF16 = jnp.bfloat16


def iota(shape, axis):
    return lax.broadcasted_iota(jnp.int32, shape, axis)


def dot(left, right, left_axis=1, right_axis=0):
    return lax.dot_general(
        left, right, (((left_axis,), (right_axis,)), ((), ())), preferred_element_type=F32
    )


def one_hot(condition):
    return jnp.where(condition, 1.0, 0.0).astype(BF16)


def pack_kernel(
    rows_hbm,
    count_hbm,
    x_hbm,
    query_hbm,
    positive_hbm,
    negative_hbm,
    out_hbm,
    joined_hbm,
    rows_ref,
    count_ref,
    x_ref,
    query_ref,
    positive_ref,
    negative_ref,
    out_ref,
    wide_ref,
    ids_ref,
    sems,
):
    places = (
        (rows_hbm, rows_ref),
        (count_hbm, count_ref),
        (x_hbm, x_ref),
        (query_hbm, query_ref),
        (positive_hbm, positive_ref),
        (negative_hbm, negative_ref),
    )
    loads = [pltpu.make_async_copy(*pair, sems.at[n]) for n, pair in enumerate(places)]
    for load in loads:
        load.start()
    peers, slots = rows_ref.shape[1:]
    nodes, width = x_ref.shape
    total = peers * slots
    row, first = iota((total, peers), 0), iota((total, peers), 1) * slots
    mine = (row >= first) & (row < first + slots)
    start = jnp.sum(jnp.where(mine, first.astype(F32), 0.0), axis=1, keepdims=True)
    place = row[:, :1].astype(F32) - start
    at_place = iota((total, slots), 1).astype(F32) == place
    peer = one_hot(mine)
    loads[0].wait()
    loads[1].wait()
    table = dot(peer, rows_ref[0].astype(F32).astype(BF16))
    index = jnp.sum(jnp.where(at_place, table, 0.0), axis=1, keepdims=True)
    count = jnp.sum(jnp.where(mine, count_ref[...].astype(F32), 0.0), axis=1, keepdims=True)
    live = place < count
    pick = one_hot(iota((total, nodes), 1).astype(F32) == index)
    for load in loads[3:]:
        load.wait()
    wide_ref[...] = jnp.zeros_like(wide_ref)
    for n, ref in enumerate((query_ref, positive_ref, negative_ref)):
        wide_ref[n : n + 1, : ref.shape[1]] = ref[...].astype(F32)
    ids_ref[...] = wide_ref[...].astype(BF16)
    ids_place = joined_hbm.at[pl.ds(nodes, ids_ref.shape[0])]
    loads[2].wait()
    stores = [
        pltpu.make_async_copy(ids_ref, ids_place, sems.at[len(loads)]),
        pltpu.make_async_copy(x_ref, joined_hbm.at[pl.ds(0, nodes)], sems.at[len(loads) + 1]),
    ]
    for store in stores:
        store.start()
    part = peers // 2
    for n in range(2):
        part_rows = slice(n * part * slots, (n + 1) * part * slots)
        out = jnp.where(live[part_rows], dot(pick[part_rows], x_ref[...]), DEAD)
        out_ref[n * part : (n + 1) * part] = out.astype(BF16).reshape(part, slots, width)
        piece = pl.ds(n * part, part)
        stores.append(
            pltpu.make_async_copy(out_ref.at[piece], out_hbm.at[piece], sems.at[len(loads) + 2 + n])
        )
        stores[-1].start()
    for store in stores:
        store.wait()


def local_kernel(columns_ref, values_ref, x_ref, target_ref, local_ref, degree_ref):
    row_blocks, tiles_row, tile = values_ref.shape[1:4]
    nodes = x_ref.shape[0]
    peers, slots = target_ref.shape[1:]

    ones = jnp.ones((tile, 128), BF16)
    for block in range(row_blocks):
        total = jnp.zeros((tile, x_ref.shape[1]), F32)
        weight = jnp.ones((tile, 128), F32)
        for t in range(tiles_row):
            first = pl.multiple_of(columns_ref[0, block, t] * tile, tile)
            values = values_ref[0, block, t]
            total += dot(values, x_ref[pl.ds(first, tile), :])
            weight += dot(values, ones)
        local_ref[block * tile : (block + 1) * tile, :] = total
        degree_ref[block * tile : (block + 1) * tile, :128] = weight

    total = peers * slots
    shape = (peers, total)
    column, first = iota(shape, 1), iota(shape, 0) * slots
    mine = (column >= first) & (column < first + slots)
    start = jnp.sum(jnp.where(mine, first.astype(F32), 0.0), axis=0, keepdims=True)
    place = iota((1, total), 1).astype(F32) - start
    spread = one_hot(iota((slots, total), 0).astype(F32) == place)
    table = dot(target_ref[0].astype(F32).astype(BF16), spread)
    target = jnp.sum(jnp.where(mine, table, 0.0), axis=0, keepdims=True)
    degree_ref[:, 128:] = jnp.where(iota((nodes, total), 0).astype(F32) == target, 1.0, 0.0)


def aggregate_kernel(received_ref, local_ref, degree_ref, out_ref):
    received = received_ref[...].astype(F32)
    live = received[:, :1] < DEAD_FLOOR
    weighted = jnp.where(live, received, 0.0).astype(BF16)
    flags = jnp.broadcast_to(jnp.where(live, 1.0, 0.0), (received.shape[0], 128)).astype(BF16)
    hot = degree_ref[:, 128:].astype(BF16)
    degree = degree_ref[:, :128] + dot(hot, flags)
    summed = local_ref[...] + dot(hot, weighted)
    width = summed.shape[1]
    for first in range(0, width, 128):
        out_ref[:, first : first + 128] = (summed[:, first : first + 128] / degree).astype(BF16)


def normed(pre):
    scale = lax.rsqrt(jnp.mean(pre * pre, axis=1, keepdims=True) + EPSILON)
    return pre * scale, scale


def columns_of(group, members, whole):
    columns = whole.shape[1] // members
    part = whole[:, :columns]
    for other in range(1, members):
        there = whole[:, other * columns : (other + 1) * columns]
        part = jnp.where(group == other, there, part)
    return part


def embed_kernel(
    members,
    sizes,
    group_ref,
    aggregate_ref,
    weight_self_ref,
    weight_neigh_ref,
    *refs,
):
    queries, negatives = sizes
    candidates = members * negatives
    joined, refs = refs[:members], refs[members:]
    (embeds_hbm, embeds_ref, part_ref, scale_ref, turned_ref), refs = refs[:5], refs[5:]
    (pair_ref, rest_ref, hot_ref), refs = refs[:3], refs[3:]
    pres, x_turned, sem = refs[: members - 1], refs[members - 1 : -1], refs[-1]
    aggregate = aggregate_ref[...]
    nodes = aggregate.shape[0]

    own_pre = dot(joined[0][:nodes], weight_self_ref[...])
    exact, scale = normed(own_pre + dot(aggregate, weight_neigh_ref[...]))
    embeds_ref[...] = exact.astype(BF16)
    copy = pltpu.make_async_copy(embeds_ref, embeds_hbm, sem)
    copy.start()
    part_ref[...] = columns_of(group_ref[0], members, exact)
    scale_ref[...] = jnp.broadcast_to(scale, scale_ref.shape)
    turned_ref[...] = aggregate.T.reshape(turned_ref.shape)

    for member, joined_ref in enumerate(joined):
        if member:
            pres[member - 1][...] = dot(joined_ref[:nodes], weight_self_ref[...])
        x_turned[member][...] = joined_ref[:nodes].T.reshape(x_turned[member].shape)
        ids = joined_ref[nodes:].astype(F32)
        query, negative = ids[:1, :queries], ids[2:3, :negatives]
        relative = ids[1:2, :queries] - (group_ref[0] * negatives).astype(F32)
        relative = jnp.where(relative < 0.0, relative + candidates, relative)
        query_hot = one_hot(iota((nodes, queries), 0).astype(F32) == query)
        positive_hot = one_hot(iota((candidates, queries), 0).astype(F32) == relative)
        pair = dot(positive_hot, query_hot, 1, 1)
        lanes = slice(member * nodes, (member + 1) * nodes)
        pair_ref[:, lanes] = pair
        rest_ref[:, lanes] = jnp.sum(pair, axis=0, keepdims=True) - pair
        square = (negatives, negatives)
        column = jnp.where(iota(square, 0) == iota(square, 1), negative, 0.0)
        column = jnp.sum(column, axis=1, keepdims=True)
        hot = one_hot(iota((negatives, nodes), 1).astype(F32) == column)
        for n in range(members):
            block = hot if n == member else jnp.zeros_like(hot)
            hot_ref[n * negatives : (n + 1) * negatives, lanes] = block
    copy.wait()


def rows_of_core(core, ref, lefts, rights):
    half, _, rows, nodes = lefts[0][0].shape
    columns = ref.shape[2]
    for part, left_refs in enumerate(lefts):
        block = jnp.zeros((half * rows, columns), F32)
        for left_ref, right in zip(left_refs, rights):
            block += dot(left_ref[:, core].reshape(half * rows, nodes), right)
        ref[part * half : (part + 1) * half] = block.reshape(half, rows, columns).astype(BF16)


def keep_kernel(core_ref, *refs):
    *refs, keep_ref = refs
    members = len(refs) // 3
    lefts = (refs[:members], refs[members : 2 * members])
    rows_of_core(core_ref[0], keep_ref, lefts, [ref[...] for ref in refs[2 * members :]])


def gradient_kernel(
    query_total,
    core_ref,
    group_ref,
    weight_neigh_ref,
    embeds_ref,
    part_ref,
    scale_ref,
    pair_ref,
    rest_ref,
    hot_ref,
    x_turned_ref,
    turned_ref,
    *refs,
):
    candidates, nodes = hot_ref.shape[0], embeds_ref.shape[0]
    members = hot_ref.shape[1] // nodes
    negatives = candidates // members
    others = members - 1
    given, refs = refs[: 3 * others], refs[3 * others :]
    send_ref, pre_grad_refs, other_turned = refs[0], refs[1 : 1 + members], refs[1 + members :]
    width = embeds_ref.shape[1]
    group = group_ref[0]
    score_factor = 1.0 / math.sqrt(width)
    factor = LOSS_FACTOR / query_total

    parts, scales, embeds = [part_ref[...]], [scale_ref[:, :1]], [embeds_ref[...]]
    x_turned, turned = [x_turned_ref], [turned_ref]
    for other, other_turned_ref in enumerate(other_turned):
        aggregate_ref, pre_ref, other_x_turned_ref = given[3 * other : 3 * other + 3]
        aggregate = aggregate_ref[...]
        exact, scale = normed(pre_ref[...] + dot(aggregate, weight_neigh_ref[...]))
        parts.append(columns_of(group, members, exact))
        scales.append(scale)
        embeds.append(exact.astype(BF16))
        other_turned_ref[...] = aggregate.T.reshape(other_turned_ref.shape)
        x_turned.append(other_x_turned_ref)
        turned.append(other_turned_ref)

    lanes = [slice(m * nodes, (m + 1) * nodes) for m in range(members)]
    hot = hot_ref[...]
    own = [hot[m * negatives : (m + 1) * negatives, lanes[m]] for m in range(members)]
    cand = jnp.concatenate([dot(own[m], embeds[m]).astype(BF16) for m in range(members)], axis=0)
    product = jnp.concatenate([dot(cand, embeds[m], 1, 1) for m in range(members)], axis=1)
    sigma = jax.nn.sigmoid(score_factor * product)
    at_positive = ((sigma - 1.0) * factor).astype(BF16).astype(F32)
    elsewhere = ((sigma / (candidates - 1.0)) * factor).astype(BF16).astype(F32)
    grad = score_factor * (rest_ref[...] * elsewhere + pair_ref[...] * at_positive)
    grad = grad.astype(BF16)
    cand_grad = sum(
        dot(grad[:, lanes[m]], parts[m].astype(BF16)) for m in range(members)
    ).astype(BF16)

    weighted = grad.astype(F32) * product
    weighted += hot.astype(F32) * jnp.sum(weighted, axis=1, keepdims=True)
    inner = jnp.sum(weighted, axis=0, keepdims=True) / width
    inner = jnp.broadcast_to(inner, (8, inner.shape[1])).T[:, :1]

    left = jnp.concatenate([grad, hot], axis=0)
    right = jnp.concatenate([columns_of(group, members, cand), cand_grad], axis=0)
    pre_grads = [
        (scales[m] * (dot(left[:, lanes[m]], right, 0, 0) - parts[m] * inner[lanes[m]])).astype(BF16)
        for m in range(members)
    ]
    for ref, pre_grad in zip(pre_grad_refs, pre_grads):
        ref[...] = pre_grad
    rows_of_core(1 - core_ref[0], send_ref, (x_turned, turned), pre_grads)


VMEM = pl.BlockSpec(memory_space=pltpu.VMEM)
SMEM = pl.BlockSpec(memory_space=pltpu.SMEM)
HBM = pl.BlockSpec(memory_space=pltpu.HBM)


def call(kernel, name, outs, args, flops=0, scratch=(), grant=16 << 20):
    shapes = [jax.ShapeDtypeStruct(shape, kind) for shape, kind, _ in outs]
    arrays = [a for a, _ in args]
    moved = sum(math.prod(a.shape) * a.dtype.itemsize for a in arrays + shapes)
    return pl.pallas_call(
        kernel,
        name=name,
        out_shape=shapes,
        in_specs=[place for _, place in args],
        out_specs=[place for _, _, place in outs],
        scratch_shapes=list(scratch),
        compiler_params=pltpu.CompilerParams(vmem_limit_bytes=grant),
        cost_estimate=pl.CostEstimate(flops=flops, bytes_accessed=moved, transcendentals=0),
    )(*arrays)


def on_device(
    features,
    tile_columns,
    tile_values,
    send_rows,
    send_count,
    ghost_target,
    query_rows,
    positive_cand,
    negative_rows,
    weight_self,
    weight_neigh,
):
    nodes, width = features.shape
    peers, slots = send_rows.shape[1:]
    total = peers * slots
    queries = query_rows.shape[1]
    negatives = negative_rows.shape[1]
    groups = lax.axis_size("group")
    others = groups - 1
    candidates = negatives * groups
    chips = peers // 2
    rows = 2 * width // peers
    half = chips // 2
    columns = width // groups
    grant = min(8 * groups, 56) << 20
    group = lax.axis_index("group").astype(jnp.int32)
    core = (lax.axis_index("dom") & 1).astype(jnp.int32)

    def of_others(own):
        return [
            lax.ppermute(own, "group", [((g + k) % groups, g) for g in range(groups)])
            for k in range(1, groups)
        ]

    id_rows = 16
    outgoing, joined = call(
        pack_kernel,
        "pack",
        [((peers, slots, width), BF16, HBM), ((nodes + id_rows, width), BF16, HBM)],
        [
            (a, HBM)
            for a in (
                send_rows, send_count, features, query_rows, positive_cand, negative_rows
            )
        ],
        flops=2 * total * nodes * width,
        scratch=[
            pltpu.VMEM(send_rows.shape, jnp.int32),
            pltpu.VMEM(send_count.shape, jnp.int32),
            pltpu.VMEM(features.shape, BF16),
            pltpu.VMEM(query_rows.shape, jnp.int32),
            pltpu.VMEM(positive_cand.shape, jnp.int32),
            pltpu.VMEM(negative_rows.shape, jnp.int32),
            pltpu.VMEM((peers, slots, width), BF16),
            pltpu.VMEM((id_rows, width), F32),
            pltpu.VMEM((id_rows, width), BF16),
            pltpu.SemaphoreType.DMA((10,)),
        ],
        grant=None,
    )
    received = lax.all_to_all(
        outgoing, "dom", split_axis=0, concat_axis=0, tiled=True
    ).reshape(total, width)

    joined = [joined] + of_others(joined)
    local, degree = call(
        local_kernel,
        "local",
        [((nodes, width), F32, VMEM), ((nodes, 128 + total), F32, VMEM)],
        [(tile_columns, SMEM), (tile_values, VMEM), (features, VMEM), (ghost_target, VMEM)],
        flops=2 * nodes * width * tile_values.shape[2] * tile_values.shape[3],
        grant=grant,
    )
    (aggregate,) = call(
        aggregate_kernel,
        "aggregate",
        [((nodes, width), BF16, VMEM)],
        [(a, VMEM) for a in (received, local, degree)],
        flops=2 * nodes * total * width,
    )
    other_aggregate = of_others(aggregate)
    node_turned = ((half, 2, rows, nodes), BF16, VMEM)
    core, group_place = core.reshape(1), (group.reshape(1), SMEM)
    embeds_out, embeds, part, scale, turned, pair, rest, hot, *made = call(
        functools.partial(embed_kernel, groups, (queries, negatives)),
        "embed",
        [
            ((nodes, width), BF16, HBM),
            ((nodes, width), BF16, VMEM),
            ((nodes, columns), F32, VMEM),
            ((nodes, 128), F32, VMEM),
            node_turned,
            ((candidates, groups * nodes), F32, VMEM),
            ((candidates, groups * nodes), F32, VMEM),
            ((candidates, groups * nodes), BF16, VMEM),
        ]
        + [((nodes, width), F32, VMEM)] * others
        + [node_turned] * groups,
        [group_place]
        + [(a, VMEM) for a in (aggregate, weight_self, weight_neigh, *joined)],
        flops=2 * nodes * width * width * groups,
        scratch=[pltpu.SemaphoreType.DMA],
        grant=grant,
    )
    x_turned, *features_turned = made[others:]
    members = []
    for trio in zip(other_aggregate, made[:others], features_turned):
        members += trio
    send, *made = call(
        functools.partial(gradient_kernel, queries),
        "gradient",
        [((chips, rows, columns), BF16, VMEM)]
        + [((nodes, columns), BF16, VMEM)] * groups
        + [node_turned] * others,
        [(core, SMEM), group_place]
        + [
            (a, VMEM)
            for a in (
                weight_neigh,
                embeds,
                part,
                scale,
                pair,
                rest,
                hot,
                x_turned,
                turned,
                *members,
            )
        ],
        flops=2 * nodes * width * width,
        grant=grant,
    )
    features_turned = [x_turned] + features_turned
    aggregates_turned = [turned] + made[groups:]
    (keep,) = call(
        keep_kernel,
        "keep",
        [((chips, rows, columns), BF16, VMEM)],
        [(core, SMEM)]
        + [(a, VMEM) for a in (*features_turned, *aggregates_turned, *made[:groups])],
        flops=2 * nodes * width * width,
        grant=grant,
    )

    swap = [(i, i ^ 1) for i in range(peers)]
    same_core = [[c + 2 * chip for chip in range(chips)] for c in range(2)]
    chip_sum = (keep.astype(F32) + lax.ppermute(send, "dom", swap).astype(F32)).astype(BF16)
    parts = lax.all_to_all(
        chip_sum,
        "dom",
        split_axis=0,
        concat_axis=0,
        axis_index_groups=same_core,
        tiled=True,
    )
    summed = jnp.sum(parts.astype(F32), axis=0).astype(BF16)
    if groups == 2:
        (other,) = of_others(summed)
        shard = jnp.where(
            group == 0,
            jnp.concatenate([summed, other], axis=1),
            jnp.concatenate([other, summed], axis=1),
        )
    else:
        shard = lax.all_gather(summed, "group", axis=1, tiled=True)
    return (embeds_out, shard)


def solution(mesh):
    placed = (
        P(("group", "dom"), None),
        P(("group", "dom"), None, None),
        P(("group", "dom"), None, None, None, None),
        P(("group", "dom"), None, None),
        P(("group", "dom"), None),
        P(("group", "dom"), None, None),
        P(("group", "dom"), None),
        P(("group", "dom"), None),
        P(("group", "dom"), None),
        P(),
        P(),
    )
    return jax.shard_map(
        on_device,
        mesh=mesh,
        in_specs=placed,
        out_specs=(P(("group", "dom"), None), P("dom", None)),
        check_vma=False,
    )
```

```python
import functools
import math

import jax
import jax.numpy as jnp
from jax import lax
from jax.experimental import pallas as pl
from jax.experimental.pallas import tpu as pltpu
from jax.sharding import PartitionSpec as P

LOSS_FACTOR = 64.0
EPSILON = 1e-05
DEAD = 256.0
DEAD_FLOOR = 128.0

F32 = jnp.float32
BF16 = jnp.bfloat16


def iota(shape, axis):
    return lax.broadcasted_iota(jnp.int32, shape, axis)


def dot(left, right, left_axis=1, right_axis=0):
    return lax.dot_general(
        left, right, (((left_axis,), (right_axis,)), ((), ())), preferred_element_type=F32
    )


def one_hot(condition):
    return jnp.where(condition, 1.0, 0.0).astype(BF16)


def pack_kernel(
    rows_hbm,
    count_hbm,
    x_hbm,
    query_hbm,
    positive_hbm,
    negative_hbm,
    out_hbm,
    joined_hbm,
    rows_ref,
    count_ref,
    x_ref,
    query_ref,
    positive_ref,
    negative_ref,
    out_ref,
    wide_ref,
    ids_ref,
    sems,
):
    places = (
        (rows_hbm, rows_ref),
        (count_hbm, count_ref),
        (x_hbm, x_ref),
        (query_hbm, query_ref),
        (positive_hbm, positive_ref),
        (negative_hbm, negative_ref),
    )
    loads = [pltpu.make_async_copy(*pair, sems.at[n]) for n, pair in enumerate(places)]
    for load in loads:
        load.start()
    peers, slots = rows_ref.shape[1:]
    nodes, width = x_ref.shape
    total = peers * slots
    row, first = iota((total, peers), 0), iota((total, peers), 1) * slots
    mine = (row >= first) & (row < first + slots)
    start = jnp.sum(jnp.where(mine, first.astype(F32), 0.0), axis=1, keepdims=True)
    place = row[:, :1].astype(F32) - start
    at_place = iota((total, slots), 1).astype(F32) == place
    peer = one_hot(mine)
    loads[0].wait()
    loads[1].wait()
    table = dot(peer, rows_ref[0].astype(F32).astype(BF16))
    index = jnp.sum(jnp.where(at_place, table, 0.0), axis=1, keepdims=True)
    count = jnp.sum(jnp.where(mine, count_ref[...].astype(F32), 0.0), axis=1, keepdims=True)
    live = place < count
    pick = one_hot(iota((total, nodes), 1).astype(F32) == index)
    for load in loads[3:]:
        load.wait()
    wide_ref[...] = jnp.zeros_like(wide_ref)
    for n, ref in enumerate((query_ref, positive_ref, negative_ref)):
        wide_ref[n : n + 1, : ref.shape[1]] = ref[...].astype(F32)
    ids_ref[...] = wide_ref[...].astype(BF16)
    ids_place = joined_hbm.at[pl.ds(nodes, ids_ref.shape[0])]
    loads[2].wait()
    stores = [
        pltpu.make_async_copy(ids_ref, ids_place, sems.at[len(loads)]),
        pltpu.make_async_copy(x_ref, joined_hbm.at[pl.ds(0, nodes)], sems.at[len(loads) + 1]),
    ]
    for store in stores:
        store.start()
    part = peers // 2
    for n in range(2):
        part_rows = slice(n * part * slots, (n + 1) * part * slots)
        out = jnp.where(live[part_rows], dot(pick[part_rows], x_ref[...]), DEAD)
        out_ref[n * part : (n + 1) * part] = out.astype(BF16).reshape(part, slots, width)
        piece = pl.ds(n * part, part)
        stores.append(
            pltpu.make_async_copy(out_ref.at[piece], out_hbm.at[piece], sems.at[len(loads) + 2 + n])
        )
        stores[-1].start()
    for store in stores:
        store.wait()


def local_kernel(columns_ref, values_ref, x_ref, target_ref, local_ref, degree_ref):
    row_blocks, tiles_row, tile = values_ref.shape[1:4]
    nodes = x_ref.shape[0]
    peers, slots = target_ref.shape[1:]

    ones = jnp.ones((tile, 128), BF16)
    for block in range(row_blocks):
        total = jnp.zeros((tile, x_ref.shape[1]), F32)
        weight = jnp.ones((tile, 128), F32)
        for t in range(tiles_row):
            first = pl.multiple_of(columns_ref[0, block, t] * tile, tile)
            values = values_ref[0, block, t]
            total += dot(values, x_ref[pl.ds(first, tile), :])
            weight += dot(values, ones)
        local_ref[block * tile : (block + 1) * tile, :] = total
        degree_ref[block * tile : (block + 1) * tile, :128] = weight

    total = peers * slots
    shape = (peers, total)
    column, first = iota(shape, 1), iota(shape, 0) * slots
    mine = (column >= first) & (column < first + slots)
    start = jnp.sum(jnp.where(mine, first.astype(F32), 0.0), axis=0, keepdims=True)
    place = iota((1, total), 1).astype(F32) - start
    spread = one_hot(iota((slots, total), 0).astype(F32) == place)
    table = dot(target_ref[0].astype(F32).astype(BF16), spread)
    target = jnp.sum(jnp.where(mine, table, 0.0), axis=0, keepdims=True)
    degree_ref[:, 128:] = jnp.where(iota((nodes, total), 0).astype(F32) == target, 1.0, 0.0)


def aggregate_kernel(received_ref, local_ref, degree_ref, head_ref, tail_ref):
    received = received_ref[...].astype(F32)
    live = received[:, :1] < DEAD_FLOOR
    weighted = jnp.where(live, received, 0.0).astype(BF16)
    flags = jnp.broadcast_to(jnp.where(live, 1.0, 0.0), (received.shape[0], 128)).astype(BF16)
    hot = degree_ref[:, 128:].astype(BF16)
    degree = degree_ref[:, :128] + dot(hot, flags)
    summed = local_ref[...] + dot(hot, weighted)
    width = summed.shape[1]
    for first in range(0, width, 128):
        mean = (summed[:, first : first + 128] / degree).astype(BF16)
        head_ref[:, first : first + 128] = mean[: head_ref.shape[0]]
        tail_ref[:, first : first + 128] = mean[head_ref.shape[0] :]


def normed(pre):
    scale = lax.rsqrt(jnp.mean(pre * pre, axis=1, keepdims=True) + EPSILON)
    return pre * scale, scale


def columns_of(group, members, whole):
    columns = whole.shape[1] // members
    part = whole[:, :columns]
    for other in range(1, members):
        there = whole[:, other * columns : (other + 1) * columns]
        part = jnp.where(group == other, there, part)
    return part


def embed_kernel(
    members,
    sizes,
    group_ref,
    head_ref,
    tail_ref,
    weight_self_ref,
    weight_neigh_ref,
    *refs,
):
    queries, negatives = sizes
    candidates = members * negatives
    joined, refs = refs[:members], refs[members:]
    (embeds_hbm, embeds_ref, part_ref, scale_ref, turned_ref), refs = refs[:5], refs[5:]
    (pair_ref, rest_ref, hot_ref), refs = refs[:3], refs[3:]
    pres, x_turned, sem = refs[: members - 1], refs[members - 1 : -1], refs[-1]
    aggregate = jnp.concatenate([head_ref[...], tail_ref[...]], axis=0)
    nodes = aggregate.shape[0]

    own_pre = dot(joined[0][:nodes], weight_self_ref[...])
    exact, scale = normed(own_pre + dot(aggregate, weight_neigh_ref[...]))
    embeds_ref[...] = exact.astype(BF16)
    copy = pltpu.make_async_copy(embeds_ref, embeds_hbm, sem)
    copy.start()
    part_ref[...] = columns_of(group_ref[0], members, exact)
    scale_ref[...] = jnp.broadcast_to(scale, scale_ref.shape)
    turned_ref[...] = aggregate.T.reshape(turned_ref.shape)

    for member, joined_ref in enumerate(joined):
        if member:
            pres[member - 1][...] = dot(joined_ref[:nodes], weight_self_ref[...])
        x_turned[member][...] = joined_ref[:nodes].T.reshape(x_turned[member].shape)
        ids = joined_ref[nodes:].astype(F32)
        query, negative = ids[:1, :queries], ids[2:3, :negatives]
        relative = ids[1:2, :queries] - (group_ref[0] * negatives).astype(F32)
        relative = jnp.where(relative < 0.0, relative + candidates, relative)
        query_hot = one_hot(iota((nodes, queries), 0).astype(F32) == query)
        positive_hot = one_hot(iota((candidates, queries), 0).astype(F32) == relative)
        pair = dot(positive_hot, query_hot, 1, 1)
        lanes = slice(member * nodes, (member + 1) * nodes)
        pair_ref[:, lanes] = pair
        rest_ref[:, lanes] = jnp.sum(pair, axis=0, keepdims=True) - pair
        square = (negatives, negatives)
        column = jnp.where(iota(square, 0) == iota(square, 1), negative, 0.0)
        column = jnp.sum(column, axis=1, keepdims=True)
        hot = one_hot(iota((negatives, nodes), 1).astype(F32) == column)
        for n in range(members):
            block = hot if n == member else jnp.zeros_like(hot)
            hot_ref[n * negatives : (n + 1) * negatives, lanes] = block
    copy.wait()


def ahead_kernel(group_ref, weight_neigh_ref, *refs):
    others = len(refs) // 6
    members = others + 1
    given, made = refs[: 2 * others], refs[2 * others :]
    for other in range(others):
        head_ref, pre_ref = given[2 * other : 2 * other + 2]
        part_ref, embeds_ref, scale_ref, turned_ref = made[4 * other : 4 * other + 4]
        aggregate = head_ref[...]
        pre = pre_ref[: aggregate.shape[0]]
        exact, scale = normed(pre + dot(aggregate, weight_neigh_ref[...]))
        part_ref[...] = columns_of(group_ref[0], members, exact)
        embeds_ref[...] = exact.astype(BF16)
        scale_ref[...] = jnp.broadcast_to(scale, scale_ref.shape)
        turned_ref[...] = aggregate.T.reshape(turned_ref.shape)


def rows_of_core(core, ref, lefts, rights):
    half, _, rows, nodes = lefts[0][0][0].shape
    columns = ref.shape[2]
    for part, left_refs in enumerate(lefts):
        block = jnp.zeros((half * rows, columns), F32)
        for pieces, right in zip(left_refs, rights):
            left = jnp.concatenate([piece[:, core] for piece in pieces], axis=2)
            block += dot(left.reshape(half * rows, nodes), right)
        ref[part * half : (part + 1) * half] = block.reshape(half, rows, columns).astype(BF16)


def keep_kernel(members, core_ref, *refs):
    *refs, keep_ref = refs
    features, refs = [(ref,) for ref in refs[:members]], refs[members:]
    rights, refs = refs[:members], refs[members:]
    aggregates = [(refs[0],)] + [refs[n : n + 2] for n in range(1, len(refs), 2)]
    rows_of_core(core_ref[0], keep_ref, (features, aggregates), [ref[...] for ref in rights])


def gradient_kernel(
    query_total,
    core_ref,
    group_ref,
    weight_neigh_ref,
    embeds_ref,
    part_ref,
    scale_ref,
    pair_ref,
    rest_ref,
    hot_ref,
    x_turned_ref,
    turned_ref,
    *refs,
):
    candidates, nodes = hot_ref.shape[0], embeds_ref.shape[0]
    members = hot_ref.shape[1] // nodes
    negatives = candidates // members
    others = members - 1
    given, refs = refs[: 7 * others], refs[7 * others :]
    send_ref, pre_grad_refs, other_turned = refs[0], refs[1 : 1 + members], refs[1 + members :]
    width = embeds_ref.shape[1]
    group = group_ref[0]
    score_factor = 1.0 / math.sqrt(width)
    factor = LOSS_FACTOR / query_total

    parts, scales, embeds = [part_ref[...]], [scale_ref[:, :1]], [embeds_ref[...]]
    x_turned, turned = [(x_turned_ref,)], [(turned_ref,)]
    for other, tail_turned_ref in enumerate(other_turned):
        tail_ref, pre_ref, other_x_turned_ref, *first = given[7 * other : 7 * other + 7]
        first_part_ref, first_embeds_ref, first_scale_ref, first_turned_ref = first
        aggregate = tail_ref[...]
        pre = pre_ref[nodes - aggregate.shape[0] :]
        exact, scale = normed(pre + dot(aggregate, weight_neigh_ref[...]))
        part = columns_of(group, members, exact)
        parts.append(jnp.concatenate([first_part_ref[...], part], axis=0))
        scales.append(jnp.concatenate([first_scale_ref[:, :1], scale], axis=0))
        embeds.append(jnp.concatenate([first_embeds_ref[...], exact.astype(BF16)], axis=0))
        x_turned.append((other_x_turned_ref,))
        turned.append((first_turned_ref, tail_turned_ref))

    lanes = [slice(m * nodes, (m + 1) * nodes) for m in range(members)]
    hot = hot_ref[...]
    own = [hot[m * negatives : (m + 1) * negatives, lanes[m]] for m in range(members)]
    cand = jnp.concatenate([dot(own[m], embeds[m]).astype(BF16) for m in range(members)], axis=0)
    product = jnp.concatenate([dot(cand, embeds[m], 1, 1) for m in range(members)], axis=1)
    sigma = jax.nn.sigmoid(score_factor * product)
    at_positive = ((sigma - 1.0) * factor).astype(BF16).astype(F32)
    elsewhere = ((sigma / (candidates - 1.0)) * factor).astype(BF16).astype(F32)
    grad = score_factor * (rest_ref[...] * elsewhere + pair_ref[...] * at_positive)
    grad = grad.astype(BF16)
    cand_grad = sum(
        dot(grad[:, lanes[m]], parts[m].astype(BF16)) for m in range(members)
    ).astype(BF16)

    weighted = grad.astype(F32) * product
    weighted += hot.astype(F32) * jnp.sum(weighted, axis=1, keepdims=True)
    inner = jnp.sum(weighted, axis=0, keepdims=True) / width
    inner = jnp.broadcast_to(inner, (8, inner.shape[1])).T[:, :1]

    left = jnp.concatenate([grad, hot], axis=0)
    right = jnp.concatenate([columns_of(group, members, cand), cand_grad], axis=0)
    pre_grads = [
        (scales[m] * (dot(left[:, lanes[m]], right, 0, 0) - parts[m] * inner[lanes[m]])).astype(BF16)
        for m in range(members)
    ]
    for other, tail_turned_ref in enumerate(other_turned):
        tail_turned_ref[...] = given[7 * other][...].T.reshape(tail_turned_ref.shape)
    for ref, pre_grad in zip(pre_grad_refs, pre_grads):
        ref[...] = pre_grad
    rows_of_core(1 - core_ref[0], send_ref, (x_turned, turned), pre_grads)


VMEM = pl.BlockSpec(memory_space=pltpu.VMEM)
SMEM = pl.BlockSpec(memory_space=pltpu.SMEM)
HBM = pl.BlockSpec(memory_space=pltpu.HBM)


def call(kernel, name, outs, args, flops=0, scratch=(), grant=16 << 20):
    shapes = [jax.ShapeDtypeStruct(shape, kind) for shape, kind, _ in outs]
    arrays = [a for a, _ in args]
    moved = sum(math.prod(a.shape) * a.dtype.itemsize for a in arrays + shapes)
    return pl.pallas_call(
        kernel,
        name=name,
        out_shape=shapes,
        in_specs=[place for _, place in args],
        out_specs=[place for _, _, place in outs],
        scratch_shapes=list(scratch),
        compiler_params=pltpu.CompilerParams(vmem_limit_bytes=grant),
        cost_estimate=pl.CostEstimate(flops=flops, bytes_accessed=moved, transcendentals=0),
    )(*arrays)


def on_device(
    features,
    tile_columns,
    tile_values,
    send_rows,
    send_count,
    ghost_target,
    query_rows,
    positive_cand,
    negative_rows,
    weight_self,
    weight_neigh,
):
    nodes, width = features.shape
    peers, slots = send_rows.shape[1:]
    total = peers * slots
    queries = query_rows.shape[1]
    negatives = negative_rows.shape[1]
    groups = lax.axis_size("group")
    others = groups - 1
    candidates = negatives * groups
    chips = peers // 2
    rows = 2 * width // peers
    half = chips // 2
    columns = width // groups
    grant = min(8 * groups, 56) << 20
    group = lax.axis_index("group").astype(jnp.int32)
    core = (lax.axis_index("dom") & 1).astype(jnp.int32)

    def of_others(own):
        return [
            lax.ppermute(own, "group", [((g + k) % groups, g) for g in range(groups)])
            for k in range(1, groups)
        ]

    id_rows = 16
    outgoing, joined = call(
        pack_kernel,
        "pack",
        [((peers, slots, width), BF16, HBM), ((nodes + id_rows, width), BF16, HBM)],
        [
            (a, HBM)
            for a in (
                send_rows, send_count, features, query_rows, positive_cand, negative_rows
            )
        ],
        flops=2 * total * nodes * width,
        scratch=[
            pltpu.VMEM(send_rows.shape, jnp.int32),
            pltpu.VMEM(send_count.shape, jnp.int32),
            pltpu.VMEM(features.shape, BF16),
            pltpu.VMEM(query_rows.shape, jnp.int32),
            pltpu.VMEM(positive_cand.shape, jnp.int32),
            pltpu.VMEM(negative_rows.shape, jnp.int32),
            pltpu.VMEM((peers, slots, width), BF16),
            pltpu.VMEM((id_rows, width), F32),
            pltpu.VMEM((id_rows, width), BF16),
            pltpu.SemaphoreType.DMA((10,)),
        ],
        grant=None,
    )
    received = lax.all_to_all(
        outgoing, "dom", split_axis=0, concat_axis=0, tiled=True
    ).reshape(total, width)

    joined = [joined] + of_others(joined)
    local, degree = call(
        local_kernel,
        "local",
        [((nodes, width), F32, VMEM), ((nodes, 128 + total), F32, VMEM)],
        [(tile_columns, SMEM), (tile_values, VMEM), (features, VMEM), (ghost_target, VMEM)],
        flops=2 * nodes * width * tile_values.shape[2] * tile_values.shape[3],
        grant=grant,
    )
    first, last = nodes // 2, nodes - nodes // 2
    head, tail = call(
        aggregate_kernel,
        "aggregate",
        [((first, width), BF16, VMEM), ((last, width), BF16, VMEM)],
        [(a, VMEM) for a in (received, local, degree)],
        flops=2 * nodes * total * width,
    )
    other_heads, other_tails = of_others(head), of_others(tail)
    node_turned = ((half, 2, rows, nodes), BF16, VMEM)
    core, group_place = core.reshape(1), (group.reshape(1), SMEM)
    embeds_out, embeds, part, scale, turned, pair, rest, hot, *made = call(
        functools.partial(embed_kernel, groups, (queries, negatives)),
        "embed",
        [
            ((nodes, width), BF16, HBM),
            ((nodes, width), BF16, VMEM),
            ((nodes, columns), F32, VMEM),
            ((nodes, 128), F32, VMEM),
            node_turned,
            ((candidates, groups * nodes), F32, VMEM),
            ((candidates, groups * nodes), F32, VMEM),
            ((candidates, groups * nodes), BF16, VMEM),
        ]
        + [((nodes, width), F32, VMEM)] * others
        + [node_turned] * groups,
        [group_place]
        + [(a, VMEM) for a in (head, tail, weight_self, weight_neigh, *joined)],
        flops=2 * nodes * width * width * groups,
        scratch=[pltpu.SemaphoreType.DMA],
        grant=grant,
    )
    x_turned, *features_turned = made[others:]
    pres = made[:others]
    ahead = call(
        ahead_kernel,
        "ahead",
        [
            ((first, columns), F32, VMEM),
            ((first, width), BF16, VMEM),
            ((first, 128), F32, VMEM),
            ((half, 2, rows, first), BF16, VMEM),
        ]
        * others,
        [group_place, (weight_neigh, VMEM)]
        + [(a, VMEM) for pair_of in zip(other_heads, pres) for a in pair_of],
        flops=2 * first * width * width,
        grant=grant,
    )
    members = []
    for n in range(others):
        members += [other_tails[n], pres[n], features_turned[n], *ahead[4 * n : 4 * n + 4]]
    send, *made = call(
        functools.partial(gradient_kernel, queries),
        "gradient",
        [((chips, rows, columns), BF16, VMEM)]
        + [((nodes, columns), BF16, VMEM)] * groups
        + [((half, 2, rows, last), BF16, VMEM)] * others,
        [(core, SMEM), group_place]
        + [
            (a, VMEM)
            for a in (
                weight_neigh,
                embeds,
                part,
                scale,
                pair,
                rest,
                hot,
                x_turned,
                turned,
                *members,
            )
        ],
        flops=2 * nodes * width * width,
        grant=grant,
    )
    pieces = [turned]
    for n in range(others):
        pieces += [ahead[4 * n + 3], made[groups + n]]
    (keep,) = call(
        functools.partial(keep_kernel, groups),
        "keep",
        [((chips, rows, columns), BF16, VMEM)],
        [(core, SMEM)]
        + [(a, VMEM) for a in (x_turned, *features_turned, *made[:groups], *pieces)],
        flops=2 * nodes * width * width,
        grant=grant,
    )

    swap = [(i, i ^ 1) for i in range(peers)]
    same_core = [[c + 2 * chip for chip in range(chips)] for c in range(2)]
    chip_sum = (keep.astype(F32) + lax.ppermute(send, "dom", swap).astype(F32)).astype(BF16)
    parts = lax.all_to_all(
        chip_sum,
        "dom",
        split_axis=0,
        concat_axis=0,
        axis_index_groups=same_core,
        tiled=True,
    )
    summed = jnp.sum(parts.astype(F32), axis=0).astype(BF16)
    if groups == 2:
        (other,) = of_others(summed)
        shard = jnp.where(
            group == 0,
            jnp.concatenate([summed, other], axis=1),
            jnp.concatenate([other, summed], axis=1),
        )
    else:
        shard = lax.all_gather(summed, "group", axis=1, tiled=True)
    return (embeds_out, shard)


def solution(mesh):
    placed = (
        P(("group", "dom"), None),
        P(("group", "dom"), None, None),
        P(("group", "dom"), None, None, None, None),
        P(("group", "dom"), None, None),
        P(("group", "dom"), None),
        P(("group", "dom"), None, None),
        P(("group", "dom"), None),
        P(("group", "dom"), None),
        P(("group", "dom"), None),
        P(),
        P(),
    )
    return jax.shard_map(
        on_device,
        mesh=mesh,
        in_specs=placed,
        out_specs=(P(("group", "dom"), None), P("dom", None)),
        check_vma=False,
    )
```

```python
import functools
import math

import jax
import jax.numpy as jnp
from jax import lax
from jax.experimental import pallas as pl
from jax.experimental.pallas import tpu as pltpu
from jax.sharding import PartitionSpec as P

LOSS_FACTOR = 64.0
EPSILON = 1e-05
DEAD = 256.0
DEAD_FLOOR = 128.0

F32 = jnp.float32
BF16 = jnp.bfloat16


def iota(shape, axis):
    return lax.broadcasted_iota(jnp.int32, shape, axis)


def dot(left, right, left_axis=1, right_axis=0):
    return lax.dot_general(
        left, right, (((left_axis,), (right_axis,)), ((), ())), preferred_element_type=F32
    )


def one_hot(condition):
    return jnp.where(condition, 1.0, 0.0).astype(BF16)


def pack_kernel(
    rows_hbm,
    count_hbm,
    x_hbm,
    query_hbm,
    positive_hbm,
    negative_hbm,
    out_hbm,
    joined_hbm,
    rows_ref,
    count_ref,
    x_ref,
    query_ref,
    positive_ref,
    negative_ref,
    out_ref,
    wide_ref,
    ids_ref,
    sems,
):
    places = (
        (rows_hbm, rows_ref),
        (count_hbm, count_ref),
        (x_hbm, x_ref),
        (query_hbm, query_ref),
        (positive_hbm, positive_ref),
        (negative_hbm, negative_ref),
    )
    loads = [pltpu.make_async_copy(*pair, sems.at[n]) for n, pair in enumerate(places)]
    for load in loads:
        load.start()
    peers, slots = rows_ref.shape[1:]
    nodes, width = x_ref.shape
    total = peers * slots
    row, first = iota((total, peers), 0), iota((total, peers), 1) * slots
    mine = (row >= first) & (row < first + slots)
    start = jnp.sum(jnp.where(mine, first.astype(F32), 0.0), axis=1, keepdims=True)
    place = row[:, :1].astype(F32) - start
    at_place = iota((total, slots), 1).astype(F32) == place
    peer = one_hot(mine)
    loads[0].wait()
    loads[1].wait()
    table = dot(peer, rows_ref[0].astype(F32).astype(BF16))
    index = jnp.sum(jnp.where(at_place, table, 0.0), axis=1, keepdims=True)
    count = jnp.sum(jnp.where(mine, count_ref[...].astype(F32), 0.0), axis=1, keepdims=True)
    live = place < count
    index = jnp.where(live, index, -1.0)
    pick = one_hot(iota((total, nodes), 1).astype(F32) == index)
    for load in loads[3:]:
        load.wait()
    wide_ref[...] = jnp.zeros_like(wide_ref)
    for n, ref in enumerate((query_ref, positive_ref, negative_ref)):
        wide_ref[n : n + 1, : ref.shape[1]] = ref[...].astype(F32)
    ids_ref[...] = wide_ref[...].astype(BF16)
    ids_place = joined_hbm.at[pl.ds(nodes, ids_ref.shape[0])]
    loads[2].wait()
    stores = [
        pltpu.make_async_copy(ids_ref, ids_place, sems.at[len(loads)]),
        pltpu.make_async_copy(x_ref, joined_hbm.at[pl.ds(0, nodes)], sems.at[len(loads) + 1]),
    ]
    for store in stores:
        store.start()
    part = peers // 2
    for n in range(2):
        part_rows = slice(n * part * slots, (n + 1) * part * slots)
        out = dot(pick[part_rows], x_ref[...])
        marked = jnp.where(live[part_rows], out[:, :128], DEAD)
        out = jnp.concatenate([marked, out[:, 128:]], axis=1)
        out_ref[n * part : (n + 1) * part] = out.astype(BF16).reshape(part, slots, width)
        piece = pl.ds(n * part, part)
        stores.append(
            pltpu.make_async_copy(out_ref.at[piece], out_hbm.at[piece], sems.at[len(loads) + 2 + n])
        )
        stores[-1].start()
    for store in stores:
        store.wait()


def local_kernel(columns_ref, values_ref, x_ref, target_ref, local_ref, degree_ref):
    row_blocks, tiles_row, tile = values_ref.shape[1:4]
    nodes = x_ref.shape[0]
    peers, slots = target_ref.shape[1:]

    ones = jnp.ones((tile, 128), BF16)
    for block in range(row_blocks):
        total = jnp.zeros((tile, x_ref.shape[1]), F32)
        weight = jnp.ones((tile, 128), F32)
        for t in range(tiles_row):
            first = pl.multiple_of(columns_ref[0, block, t] * tile, tile)
            values = values_ref[0, block, t]
            total += dot(values, x_ref[pl.ds(first, tile), :])
            weight += dot(values, ones)
        local_ref[block * tile : (block + 1) * tile, :] = total
        degree_ref[block * tile : (block + 1) * tile, :128] = weight

    total = peers * slots
    shape = (peers, total)
    column, first = iota(shape, 1), iota(shape, 0) * slots
    mine = (column >= first) & (column < first + slots)
    start = jnp.sum(jnp.where(mine, first.astype(F32), 0.0), axis=0, keepdims=True)
    place = iota((1, total), 1).astype(F32) - start
    spread = one_hot(iota((slots, total), 0).astype(F32) == place)
    table = dot(target_ref[0].astype(F32).astype(BF16), spread)
    target = jnp.sum(jnp.where(mine, table, 0.0), axis=0, keepdims=True)
    degree_ref[:, 128:] = jnp.where(iota((nodes, total), 0).astype(F32) == target, 1.0, 0.0)


def aggregate_kernel(first, received_ref, local_ref, degree_ref, out_ref):
    nodes = pl.ds(first, out_ref.shape[0])
    received = received_ref[...]
    marked = received[:, :128].astype(F32)
    live = marked[:, :1] < DEAD_FLOOR
    marked = jnp.where(live, marked, 0.0).astype(BF16)
    weighted = jnp.concatenate([marked, received[:, 128:]], axis=1)
    flags = jnp.broadcast_to(jnp.where(live, 1.0, 0.0), (received.shape[0], 128)).astype(BF16)
    hot = degree_ref[nodes, 128:].astype(BF16)
    degree = degree_ref[nodes, :128] + dot(hot, flags)
    summed = local_ref[nodes, :] + dot(hot, weighted)
    for lane in range(0, summed.shape[1], 128):
        out_ref[:, lane : lane + 128] = (summed[:, lane : lane + 128] / degree).astype(BF16)


def normed(pre):
    scale = lax.rsqrt(jnp.mean(pre * pre, axis=1, keepdims=True) + EPSILON)
    return pre * scale, scale


def columns_of(group, members, whole):
    columns = whole.shape[1] // members
    part = whole[:, :columns]
    for other in range(1, members):
        there = whole[:, other * columns : (other + 1) * columns]
        part = jnp.where(group == other, there, part)
    return part


def embed_kernel(
    members,
    sizes,
    group_ref,
    head_ref,
    tail_ref,
    weight_self_ref,
    weight_neigh_ref,
    *refs,
):
    queries, negatives = sizes
    candidates = members * negatives
    joined, refs = refs[:members], refs[members:]
    (embeds_hbm, embeds_ref, part_ref, scale_ref, turned_ref), refs = refs[:5], refs[5:]
    (pair_ref, rest_ref, hot_ref), refs = refs[:3], refs[3:]
    pres, x_turned, sem = refs[: members - 1], refs[members - 1 : -1], refs[-1]
    aggregate = jnp.concatenate([head_ref[...], tail_ref[...]], axis=0)
    nodes = aggregate.shape[0]

    own_pre = dot(joined[0][:nodes], weight_self_ref[...])
    exact, scale = normed(own_pre + dot(aggregate, weight_neigh_ref[...]))
    embeds_ref[...] = exact.astype(BF16)
    copy = pltpu.make_async_copy(embeds_ref, embeds_hbm, sem)
    copy.start()
    part_ref[...] = columns_of(group_ref[0], members, exact)
    scale_ref[...] = jnp.broadcast_to(scale, scale_ref.shape)
    turned_ref[...] = aggregate.T.reshape(turned_ref.shape)

    for member, joined_ref in enumerate(joined):
        if member:
            pres[member - 1][...] = dot(joined_ref[:nodes], weight_self_ref[...])
        x_turned[member][...] = joined_ref[:nodes].T.reshape(x_turned[member].shape)
        ids = joined_ref[nodes:].astype(F32)
        query, negative = ids[:1, :queries], ids[2:3, :negatives]
        relative = ids[1:2, :queries] - (group_ref[0] * negatives).astype(F32)
        relative = jnp.where(relative < 0.0, relative + candidates, relative)
        query_hot = one_hot(iota((nodes, queries), 0).astype(F32) == query)
        positive_hot = one_hot(iota((candidates, queries), 0).astype(F32) == relative)
        pair = dot(positive_hot, query_hot, 1, 1)
        lanes = slice(member * nodes, (member + 1) * nodes)
        pair_ref[:, lanes] = pair
        rest_ref[:, lanes] = jnp.sum(pair, axis=0, keepdims=True) - pair
        square = (negatives, negatives)
        column = jnp.where(iota(square, 0) == iota(square, 1), negative, 0.0)
        column = jnp.sum(column, axis=1, keepdims=True)
        hot = one_hot(iota((negatives, nodes), 1).astype(F32) == column)
        for n in range(members):
            block = hot if n == member else jnp.zeros_like(hot)
            hot_ref[n * negatives : (n + 1) * negatives, lanes] = block
    copy.wait()


def ahead_kernel(group_ref, weight_neigh_ref, *refs):
    others = len(refs) // 6
    members = others + 1
    given, made = refs[: 2 * others], refs[2 * others :]
    for other in range(others):
        head_ref, pre_ref = given[2 * other : 2 * other + 2]
        part_ref, embeds_ref, scale_ref, turned_ref = made[4 * other : 4 * other + 4]
        aggregate = head_ref[...]
        pre = pre_ref[: aggregate.shape[0]]
        exact, scale = normed(pre + dot(aggregate, weight_neigh_ref[...]))
        part_ref[...] = columns_of(group_ref[0], members, exact)
        embeds_ref[...] = exact.astype(BF16)
        scale_ref[...] = jnp.broadcast_to(scale, scale_ref.shape)
        turned_ref[...] = aggregate.T.reshape(turned_ref.shape)


def rows_of_core(core, ref, lefts, rights):
    half, _, rows, nodes = lefts[0][0][0].shape
    columns = ref.shape[2]
    for part, left_refs in enumerate(lefts):
        block = jnp.zeros((half * rows, columns), F32)
        for pieces, right in zip(left_refs, rights):
            left = jnp.concatenate([piece[:, core] for piece in pieces], axis=2)
            block += dot(left.reshape(half * rows, nodes), right)
        ref[part * half : (part + 1) * half] = block.reshape(half, rows, columns).astype(BF16)


def keep_kernel(members, core_ref, *refs):
    *refs, keep_ref = refs
    features, refs = [(ref,) for ref in refs[:members]], refs[members:]
    rights, refs = refs[:members], refs[members:]
    aggregates = [(refs[0],)] + [refs[n : n + 2] for n in range(1, len(refs), 2)]
    rows_of_core(core_ref[0], keep_ref, (features, aggregates), [ref[...] for ref in rights])


def gradient_kernel(
    query_total,
    core_ref,
    group_ref,
    weight_neigh_ref,
    embeds_ref,
    part_ref,
    scale_ref,
    pair_ref,
    rest_ref,
    hot_ref,
    x_turned_ref,
    turned_ref,
    *refs,
):
    candidates, nodes = hot_ref.shape[0], embeds_ref.shape[0]
    members = hot_ref.shape[1] // nodes
    negatives = candidates // members
    others = members - 1
    given, refs = refs[: 7 * others], refs[7 * others :]
    send_ref, pre_grad_refs, other_turned = refs[0], refs[1 : 1 + members], refs[1 + members :]
    width = embeds_ref.shape[1]
    group = group_ref[0]
    score_factor = 1.0 / math.sqrt(width)
    factor = LOSS_FACTOR / query_total

    parts, scales, embeds = [part_ref[...]], [scale_ref[:, :1]], [embeds_ref[...]]
    x_turned, turned = [(x_turned_ref,)], [(turned_ref,)]
    for other, tail_turned_ref in enumerate(other_turned):
        tail_ref, pre_ref, other_x_turned_ref, *first = given[7 * other : 7 * other + 7]
        first_part_ref, first_embeds_ref, first_scale_ref, first_turned_ref = first
        aggregate = tail_ref[...]
        pre = pre_ref[nodes - aggregate.shape[0] :]
        exact, scale = normed(pre + dot(aggregate, weight_neigh_ref[...]))
        part = columns_of(group, members, exact)
        parts.append(jnp.concatenate([first_part_ref[...], part], axis=0))
        scales.append(jnp.concatenate([first_scale_ref[:, :1], scale], axis=0))
        embeds.append(jnp.concatenate([first_embeds_ref[...], exact.astype(BF16)], axis=0))
        x_turned.append((other_x_turned_ref,))
        turned.append((first_turned_ref, tail_turned_ref))

    lanes = [slice(m * nodes, (m + 1) * nodes) for m in range(members)]
    hot = hot_ref[...]
    own = [hot[m * negatives : (m + 1) * negatives, lanes[m]] for m in range(members)]
    cand = jnp.concatenate([dot(own[m], embeds[m]).astype(BF16) for m in range(members)], axis=0)
    product = jnp.concatenate([dot(cand, embeds[m], 1, 1) for m in range(members)], axis=1)
    sigma = jax.nn.sigmoid(score_factor * product)
    at_positive = ((sigma - 1.0) * factor).astype(BF16).astype(F32)
    elsewhere = ((sigma / (candidates - 1.0)) * factor).astype(BF16).astype(F32)
    grad = score_factor * (rest_ref[...] * elsewhere + pair_ref[...] * at_positive)
    grad = grad.astype(BF16)
    cand_grad = sum(
        dot(grad[:, lanes[m]], parts[m].astype(BF16)) for m in range(members)
    ).astype(BF16)

    weighted = grad.astype(F32) * product
    weighted += hot.astype(F32) * jnp.sum(weighted, axis=1, keepdims=True)
    inner = jnp.sum(weighted, axis=0, keepdims=True) / width
    inner = jnp.broadcast_to(inner, (8, inner.shape[1])).T[:, :1]

    left = jnp.concatenate([grad, hot], axis=0)
    right = jnp.concatenate([columns_of(group, members, cand), cand_grad], axis=0)
    pre_grads = [
        (scales[m] * (dot(left[:, lanes[m]], right, 0, 0) - parts[m] * inner[lanes[m]])).astype(BF16)
        for m in range(members)
    ]
    for other, tail_turned_ref in enumerate(other_turned):
        tail_turned_ref[...] = given[7 * other][...].T.reshape(tail_turned_ref.shape)
    for ref, pre_grad in zip(pre_grad_refs, pre_grads):
        ref[...] = pre_grad
    rows_of_core(1 - core_ref[0], send_ref, (x_turned, turned), pre_grads)


VMEM = pl.BlockSpec(memory_space=pltpu.VMEM)
SMEM = pl.BlockSpec(memory_space=pltpu.SMEM)
HBM = pl.BlockSpec(memory_space=pltpu.HBM)


def call(kernel, name, outs, args, flops=0, scratch=(), grant=16 << 20):
    shapes = [jax.ShapeDtypeStruct(shape, kind) for shape, kind, _ in outs]
    arrays = [a for a, _ in args]
    moved = sum(math.prod(a.shape) * a.dtype.itemsize for a in arrays + shapes)
    return pl.pallas_call(
        kernel,
        name=name,
        out_shape=shapes,
        in_specs=[place for _, place in args],
        out_specs=[place for _, _, place in outs],
        scratch_shapes=list(scratch),
        compiler_params=pltpu.CompilerParams(vmem_limit_bytes=grant),
        cost_estimate=pl.CostEstimate(flops=flops, bytes_accessed=moved, transcendentals=0),
    )(*arrays)


def on_device(
    features,
    tile_columns,
    tile_values,
    send_rows,
    send_count,
    ghost_target,
    query_rows,
    positive_cand,
    negative_rows,
    weight_self,
    weight_neigh,
):
    nodes, width = features.shape
    peers, slots = send_rows.shape[1:]
    total = peers * slots
    queries = query_rows.shape[1]
    negatives = negative_rows.shape[1]
    groups = lax.axis_size("group")
    others = groups - 1
    candidates = negatives * groups
    chips = peers // 2
    rows = 2 * width // peers
    half = chips // 2
    columns = width // groups
    grant = min(8 * groups, 56) << 20
    group = lax.axis_index("group").astype(jnp.int32)
    core = (lax.axis_index("dom") & 1).astype(jnp.int32)

    def of_others(own):
        return [
            lax.ppermute(own, "group", [((g + k) % groups, g) for g in range(groups)])
            for k in range(1, groups)
        ]

    id_rows = 16
    outgoing, joined = call(
        pack_kernel,
        "pack",
        [((peers, slots, width), BF16, HBM), ((nodes + id_rows, width), BF16, HBM)],
        [
            (a, HBM)
            for a in (
                send_rows, send_count, features, query_rows, positive_cand, negative_rows
            )
        ],
        flops=2 * total * nodes * width,
        scratch=[
            pltpu.VMEM(send_rows.shape, jnp.int32),
            pltpu.VMEM(send_count.shape, jnp.int32),
            pltpu.VMEM(features.shape, BF16),
            pltpu.VMEM(query_rows.shape, jnp.int32),
            pltpu.VMEM(positive_cand.shape, jnp.int32),
            pltpu.VMEM(negative_rows.shape, jnp.int32),
            pltpu.VMEM((peers, slots, width), BF16),
            pltpu.VMEM((id_rows, width), F32),
            pltpu.VMEM((id_rows, width), BF16),
            pltpu.SemaphoreType.DMA((10,)),
        ],
        grant=None,
    )
    received = lax.all_to_all(
        outgoing, "dom", split_axis=0, concat_axis=0, tiled=True
    ).reshape(total, width)

    joined = [joined] + of_others(joined)
    local, degree = call(
        local_kernel,
        "local",
        [((nodes, width), F32, VMEM), ((nodes, 128 + total), F32, VMEM)],
        [(tile_columns, SMEM), (tile_values, VMEM), (features, VMEM), (ghost_target, VMEM)],
        flops=2 * nodes * width * tile_values.shape[2] * tile_values.shape[3],
        grant=grant,
    )
    first, last = nodes // 2, nodes - nodes // 2
    head, tail = (
        call(
            functools.partial(aggregate_kernel, start),
            "aggregate",
            [((count, width), BF16, VMEM)],
            [(a, VMEM) for a in (received, local, degree)],
            flops=2 * count * total * width,
        )[0]
        for start, count in ((0, first), (first, last))
    )
    other_heads, other_tails = of_others(head), of_others(tail)
    node_turned = ((half, 2, rows, nodes), BF16, VMEM)
    core, group_place = core.reshape(1), (group.reshape(1), SMEM)
    embeds_out, embeds, part, scale, turned, pair, rest, hot, *made = call(
        functools.partial(embed_kernel, groups, (queries, negatives)),
        "embed",
        [
            ((nodes, width), BF16, HBM),
            ((nodes, width), BF16, VMEM),
            ((nodes, columns), F32, VMEM),
            ((nodes, 128), F32, VMEM),
            node_turned,
            ((candidates, groups * nodes), F32, VMEM),
            ((candidates, groups * nodes), F32, VMEM),
            ((candidates, groups * nodes), BF16, VMEM),
        ]
        + [((nodes, width), F32, VMEM)] * others
        + [node_turned] * groups,
        [group_place]
        + [(a, VMEM) for a in (head, tail, weight_self, weight_neigh, *joined)],
        flops=2 * nodes * width * width * groups,
        scratch=[pltpu.SemaphoreType.DMA],
        grant=grant,
    )
    x_turned, *features_turned = made[others:]
    pres = made[:others]
    ahead = call(
        ahead_kernel,
        "ahead",
        [
            ((first, columns), F32, VMEM),
            ((first, width), BF16, VMEM),
            ((first, 128), F32, VMEM),
            ((half, 2, rows, first), BF16, VMEM),
        ]
        * others,
        [group_place, (weight_neigh, VMEM)]
        + [(a, VMEM) for pair_of in zip(other_heads, pres) for a in pair_of],
        flops=2 * first * width * width,
        grant=grant,
    )
    members = []
    for n in range(others):
        members += [other_tails[n], pres[n], features_turned[n], *ahead[4 * n : 4 * n + 4]]
    send, *made = call(
        functools.partial(gradient_kernel, queries),
        "gradient",
        [((chips, rows, columns), BF16, VMEM)]
        + [((nodes, columns), BF16, VMEM)] * groups
        + [((half, 2, rows, last), BF16, VMEM)] * others,
        [(core, SMEM), group_place]
        + [
            (a, VMEM)
            for a in (
                weight_neigh,
                embeds,
                part,
                scale,
                pair,
                rest,
                hot,
                x_turned,
                turned,
                *members,
            )
        ],
        flops=2 * nodes * width * width,
        grant=grant,
    )
    pieces = [turned]
    for n in range(others):
        pieces += [ahead[4 * n + 3], made[groups + n]]
    (keep,) = call(
        functools.partial(keep_kernel, groups),
        "keep",
        [((chips, rows, columns), BF16, VMEM)],
        [(core, SMEM)]
        + [(a, VMEM) for a in (x_turned, *features_turned, *made[:groups], *pieces)],
        flops=2 * nodes * width * width,
        grant=grant,
    )

    swap = [(i, i ^ 1) for i in range(peers)]
    same_core = [[c + 2 * chip for chip in range(chips)] for c in range(2)]
    chip_sum = (keep.astype(F32) + lax.ppermute(send, "dom", swap).astype(F32)).astype(BF16)
    parts = lax.all_to_all(
        chip_sum,
        "dom",
        split_axis=0,
        concat_axis=0,
        axis_index_groups=same_core,
        tiled=True,
    )
    summed = jnp.sum(parts.astype(F32), axis=0).astype(BF16)
    if groups == 2:
        (other,) = of_others(summed)
        shard = jnp.where(
            group == 0,
            jnp.concatenate([summed, other], axis=1),
            jnp.concatenate([other, summed], axis=1),
        )
    else:
        shard = lax.all_gather(summed, "group", axis=1, tiled=True)
    return (embeds_out, shard)


def solution(mesh):
    placed = (
        P(("group", "dom"), None),
        P(("group", "dom"), None, None),
        P(("group", "dom"), None, None, None, None),
        P(("group", "dom"), None, None),
        P(("group", "dom"), None),
        P(("group", "dom"), None, None),
        P(("group", "dom"), None),
        P(("group", "dom"), None),
        P(("group", "dom"), None),
        P(),
        P(),
    )
    return jax.shard_map(
        on_device,
        mesh=mesh,
        in_specs=placed,
        out_specs=(P(("group", "dom"), None), P("dom", None)),
        check_vma=False,
    )
```

```python
import functools
import math

import jax
import jax.numpy as jnp
from jax import lax
from jax.experimental import pallas as pl
from jax.experimental.pallas import tpu as pltpu
from jax.sharding import PartitionSpec as P

LOSS_FACTOR = 64.0
EPSILON = 1e-05
DEAD = 256.0
DEAD_FLOOR = 128.0

F32 = jnp.float32
BF16 = jnp.bfloat16


def iota(shape, axis):
    return lax.broadcasted_iota(jnp.int32, shape, axis)


def dot(left, right, left_axis=1, right_axis=0):
    return lax.dot_general(
        left, right, (((left_axis,), (right_axis,)), ((), ())), preferred_element_type=F32
    )


def one_hot(condition):
    return jnp.where(condition, 1.0, 0.0).astype(BF16)


def pack_kernel(
    rows_hbm,
    count_hbm,
    x_hbm,
    query_hbm,
    positive_hbm,
    negative_hbm,
    out_hbm,
    joined_hbm,
    rows_ref,
    count_ref,
    x_ref,
    query_ref,
    positive_ref,
    negative_ref,
    out_ref,
    wide_ref,
    ids_ref,
    sems,
):
    places = (
        (rows_hbm, rows_ref),
        (count_hbm, count_ref),
        (x_hbm, x_ref),
        (query_hbm, query_ref),
        (positive_hbm, positive_ref),
        (negative_hbm, negative_ref),
    )
    loads = [pltpu.make_async_copy(*pair, sems.at[n]) for n, pair in enumerate(places)]
    for load in loads:
        load.start()
    peers, slots = rows_ref.shape[1:]
    nodes, width = x_ref.shape
    total = peers * slots
    row, first = iota((total, peers), 0), iota((total, peers), 1) * slots
    mine = (row >= first) & (row < first + slots)
    start = jnp.sum(jnp.where(mine, first.astype(F32), 0.0), axis=1, keepdims=True)
    place = row[:, :1].astype(F32) - start
    at_place = iota((total, slots), 1).astype(F32) == place
    peer = one_hot(mine)
    loads[0].wait()
    loads[1].wait()
    table = dot(peer, rows_ref[0].astype(F32).astype(BF16))
    index = jnp.sum(jnp.where(at_place, table, 0.0), axis=1, keepdims=True)
    count = jnp.sum(jnp.where(mine, count_ref[...].astype(F32), 0.0), axis=1, keepdims=True)
    live = place < count
    index = jnp.where(live, index, -1.0)
    pick = one_hot(iota((total, nodes), 1).astype(F32) == index)
    for load in loads[3:]:
        load.wait()
    wide_ref[...] = jnp.zeros_like(wide_ref)
    for n, ref in enumerate((query_ref, positive_ref, negative_ref)):
        wide_ref[n : n + 1, : ref.shape[1]] = ref[...].astype(F32)
    ids_ref[...] = wide_ref[...].astype(BF16)
    ids_place = joined_hbm.at[pl.ds(nodes, ids_ref.shape[0])]
    loads[2].wait()
    stores = [
        pltpu.make_async_copy(ids_ref, ids_place, sems.at[len(loads)]),
        pltpu.make_async_copy(x_ref, joined_hbm.at[pl.ds(0, nodes)], sems.at[len(loads) + 1]),
    ]
    for store in stores:
        store.start()
    part = peers // 2
    for n in range(2):
        part_rows = slice(n * part * slots, (n + 1) * part * slots)
        out = dot(pick[part_rows], x_ref[...])
        marked = jnp.where(live[part_rows], out[:, :128], DEAD)
        out = jnp.concatenate([marked, out[:, 128:]], axis=1)
        out_ref[n * part : (n + 1) * part] = out.astype(BF16).reshape(part, slots, width)
        piece = pl.ds(n * part, part)
        stores.append(
            pltpu.make_async_copy(out_ref.at[piece], out_hbm.at[piece], sems.at[len(loads) + 2 + n])
        )
        stores[-1].start()
    for store in stores:
        store.wait()


def local_kernel(columns_ref, values_ref, x_ref, target_ref, local_ref, degree_ref):
    row_blocks, tiles_row, tile = values_ref.shape[1:4]
    nodes = x_ref.shape[0]
    peers, slots = target_ref.shape[1:]

    ones = jnp.ones((tile, 128), BF16)
    for block in range(row_blocks):
        total = jnp.zeros((tile, x_ref.shape[1]), F32)
        weight = jnp.ones((tile, 128), F32)
        for t in range(tiles_row):
            first = pl.multiple_of(columns_ref[0, block, t] * tile, tile)
            values = values_ref[0, block, t]
            total += dot(values, x_ref[pl.ds(first, tile), :])
            weight += dot(values, ones)
        local_ref[block * tile : (block + 1) * tile, :] = total
        degree_ref[block * tile : (block + 1) * tile, :128] = weight

    total = peers * slots
    shape = (peers, total)
    column, first = iota(shape, 1), iota(shape, 0) * slots
    mine = (column >= first) & (column < first + slots)
    start = jnp.sum(jnp.where(mine, first.astype(F32), 0.0), axis=0, keepdims=True)
    place = iota((1, total), 1).astype(F32) - start
    spread = one_hot(iota((slots, total), 0).astype(F32) == place)
    table = dot(target_ref[0].astype(F32).astype(BF16), spread)
    target = jnp.sum(jnp.where(mine, table, 0.0), axis=0, keepdims=True)
    degree_ref[:, 128:] = jnp.where(iota((nodes, total), 0).astype(F32) == target, 1.0, 0.0)


def aggregate_kernel(first, received_ref, local_ref, degree_ref, out_ref):
    nodes = pl.ds(first, out_ref.shape[0])
    received = received_ref[...]
    marked = received[:, :128].astype(F32)
    live = marked[:, :1] < DEAD_FLOOR
    marked = jnp.where(live, marked, 0.0).astype(BF16)
    weighted = jnp.concatenate([marked, received[:, 128:]], axis=1)
    flags = jnp.broadcast_to(jnp.where(live, 1.0, 0.0), (received.shape[0], 128)).astype(BF16)
    hot = degree_ref[nodes, 128:].astype(BF16)
    degree = degree_ref[nodes, :128] + dot(hot, flags)
    summed = local_ref[nodes, :] + dot(hot, weighted)
    for lane in range(0, summed.shape[1], 128):
        out_ref[:, lane : lane + 128] = (summed[:, lane : lane + 128] / degree).astype(BF16)


def normed(pre):
    scale = lax.rsqrt(jnp.mean(pre * pre, axis=1, keepdims=True) + EPSILON)
    return pre * scale, scale


def columns_of(group, members, whole):
    columns = whole.shape[1] // members
    part = whole[:, :columns]
    for other in range(1, members):
        there = whole[:, other * columns : (other + 1) * columns]
        part = jnp.where(group == other, there, part)
    return part


def embed_kernel(
    members,
    sizes,
    group_ref,
    head_ref,
    tail_ref,
    weight_self_ref,
    weight_neigh_ref,
    *refs,
):
    queries, negatives = sizes
    candidates = members * negatives
    joined, refs = refs[:members], refs[members:]
    (embeds_hbm, embeds_ref, part_ref, scale_ref, turned_ref), refs = refs[:5], refs[5:]
    (pair_ref, rest_ref, hot_ref), refs = refs[:3], refs[3:]
    pres, x_turned, sem = refs[: members - 1], refs[members - 1 : -1], refs[-1]
    aggregate = jnp.concatenate([head_ref[...], tail_ref[...]], axis=0)
    nodes = aggregate.shape[0]

    own_pre = dot(joined[0][:nodes], weight_self_ref[...])
    exact, scale = normed(own_pre + dot(aggregate, weight_neigh_ref[...]))
    embeds_ref[...] = exact.astype(BF16)
    copy = pltpu.make_async_copy(embeds_ref, embeds_hbm, sem)
    copy.start()
    part_ref[...] = columns_of(group_ref[0], members, exact)
    scale_ref[...] = jnp.broadcast_to(scale, scale_ref.shape)
    turned_ref[...] = aggregate.T.reshape(turned_ref.shape)

    for member, joined_ref in enumerate(joined):
        if member:
            pres[member - 1][...] = dot(joined_ref[:nodes], weight_self_ref[...])
        x_turned[member][...] = joined_ref[:nodes].T.reshape(x_turned[member].shape)
        ids = joined_ref[nodes:].astype(F32)
        query, negative = ids[:1, :queries], ids[2:3, :negatives]
        relative = ids[1:2, :queries] - (group_ref[0] * negatives).astype(F32)
        relative = jnp.where(relative < 0.0, relative + candidates, relative)
        query_hot = one_hot(iota((nodes, queries), 0).astype(F32) == query)
        positive_hot = one_hot(iota((candidates, queries), 0).astype(F32) == relative)
        pair = dot(positive_hot, query_hot, 1, 1)
        lanes = slice(member * nodes, (member + 1) * nodes)
        pair_ref[:, lanes] = pair
        rest_ref[:, lanes] = jnp.sum(pair, axis=0, keepdims=True) - pair
        square = (negatives, negatives)
        column = jnp.where(iota(square, 0) == iota(square, 1), negative, 0.0)
        column = jnp.sum(column, axis=1, keepdims=True)
        hot = one_hot(iota((negatives, nodes), 1).astype(F32) == column)
        for n in range(members):
            block = hot if n == member else jnp.zeros_like(hot)
            hot_ref[n * negatives : (n + 1) * negatives, lanes] = block
    copy.wait()


def ahead_kernel(group_ref, weight_neigh_ref, *refs):
    others = len(refs) // 6
    members = others + 1
    given, made = refs[: 2 * others], refs[2 * others :]
    for other in range(others):
        head_ref, pre_ref = given[2 * other : 2 * other + 2]
        part_ref, embeds_ref, scale_ref, turned_ref = made[4 * other : 4 * other + 4]
        aggregate = head_ref[...]
        pre = pre_ref[: aggregate.shape[0]]
        exact, scale = normed(pre + dot(aggregate, weight_neigh_ref[...]))
        part_ref[...] = columns_of(group_ref[0], members, exact)
        embeds_ref[...] = exact.astype(BF16)
        scale_ref[...] = jnp.broadcast_to(scale, scale_ref.shape)
        turned_ref[...] = aggregate.T.reshape(turned_ref.shape)


def rows_of_core(core, ref, lefts, rights):
    half, _, rows, nodes = lefts[0][0][0].shape
    columns = ref.shape[2]
    for part, left_refs in enumerate(lefts):
        block = jnp.zeros((half * rows, columns), F32)
        for pieces, right in zip(left_refs, rights):
            left = jnp.concatenate([piece[:, core] for piece in pieces], axis=2)
            block += dot(left.reshape(half * rows, nodes), right)
        ref[part * half : (part + 1) * half] = block.reshape(half, rows, columns).astype(BF16)


def keep_kernel(members, core_ref, *refs):
    *refs, keep_ref = refs
    features, refs = [(ref,) for ref in refs[:members]], refs[members:]
    rights, refs = refs[:members], refs[members:]
    aggregates = [(refs[0],)] + [refs[n : n + 2] for n in range(1, len(refs), 2)]
    rows_of_core(core_ref[0], keep_ref, (features, aggregates), [ref[...] for ref in rights])


def gradient_kernel(
    query_total,
    core_ref,
    group_ref,
    weight_neigh_ref,
    embeds_ref,
    part_ref,
    scale_ref,
    pair_ref,
    rest_ref,
    hot_ref,
    x_turned_ref,
    turned_ref,
    *refs,
):
    candidates, nodes = hot_ref.shape[0], embeds_ref.shape[0]
    members = hot_ref.shape[1] // nodes
    negatives = candidates // members
    others = members - 1
    given, refs = refs[: 7 * others], refs[7 * others :]
    send_ref, pre_grad_refs, other_turned = refs[0], refs[1 : 1 + members], refs[1 + members :]
    width = embeds_ref.shape[1]
    group = group_ref[0]
    score_factor = 1.0 / math.sqrt(width)
    factor = LOSS_FACTOR / query_total

    parts, scales, embeds = [part_ref[...]], [scale_ref[:, :1]], [embeds_ref[...]]
    x_turned, turned = [(x_turned_ref,)], [(turned_ref,)]
    for other, tail_turned_ref in enumerate(other_turned):
        tail_ref, pre_ref, other_x_turned_ref, *first = given[7 * other : 7 * other + 7]
        first_part_ref, first_embeds_ref, first_scale_ref, first_turned_ref = first
        aggregate = tail_ref[...]
        pre = pre_ref[nodes - aggregate.shape[0] :]
        exact, scale = normed(pre + dot(aggregate, weight_neigh_ref[...]))
        part = columns_of(group, members, exact)
        parts.append(jnp.concatenate([first_part_ref[...], part], axis=0))
        scales.append(jnp.concatenate([first_scale_ref[:, :1], scale], axis=0))
        embeds.append(jnp.concatenate([first_embeds_ref[...], exact.astype(BF16)], axis=0))
        x_turned.append((other_x_turned_ref,))
        turned.append((first_turned_ref, tail_turned_ref))

    lanes = [slice(m * nodes, (m + 1) * nodes) for m in range(members)]
    hot = hot_ref[...]
    own = [hot[m * negatives : (m + 1) * negatives, lanes[m]] for m in range(members)]
    cand = jnp.concatenate([dot(own[m], embeds[m]).astype(BF16) for m in range(members)], axis=0)
    product = jnp.concatenate([dot(cand, embeds[m], 1, 1) for m in range(members)], axis=1)
    sigma = jax.nn.sigmoid(score_factor * product)
    at_positive = ((sigma - 1.0) * factor).astype(BF16).astype(F32)
    elsewhere = ((sigma / (candidates - 1.0)) * factor).astype(BF16).astype(F32)
    grad = score_factor * (rest_ref[...] * elsewhere + pair_ref[...] * at_positive)
    grad = grad.astype(BF16)
    cand_grad = sum(
        dot(grad[:, lanes[m]], parts[m].astype(BF16)) for m in range(members)
    ).astype(BF16)

    left = jnp.concatenate([grad, hot], axis=0)
    right = jnp.concatenate([columns_of(group, members, cand), cand_grad], axis=0)
    emb_grads = [dot(left[:, lanes[m]], right, 0, 0) for m in range(members)]

    weighted = grad.astype(F32) * product
    weighted += hot.astype(F32) * jnp.sum(weighted, axis=1, keepdims=True)
    inner = jnp.sum(weighted, axis=0, keepdims=True) / width
    inner = jnp.broadcast_to(inner, (8, inner.shape[1])).T[:, :1]

    pre_grads = [
        (scales[m] * (emb_grads[m] - parts[m] * inner[lanes[m]])).astype(BF16)
        for m in range(members)
    ]
    for other, tail_turned_ref in enumerate(other_turned):
        tail_turned_ref[...] = given[7 * other][...].T.reshape(tail_turned_ref.shape)
    for ref, pre_grad in zip(pre_grad_refs, pre_grads):
        ref[...] = pre_grad
    rows_of_core(1 - core_ref[0], send_ref, (x_turned, turned), pre_grads)


VMEM = pl.BlockSpec(memory_space=pltpu.VMEM)
SMEM = pl.BlockSpec(memory_space=pltpu.SMEM)
HBM = pl.BlockSpec(memory_space=pltpu.HBM)


def call(kernel, name, outs, args, flops=0, scratch=(), grant=16 << 20):
    shapes = [jax.ShapeDtypeStruct(shape, kind) for shape, kind, _ in outs]
    arrays = [a for a, _ in args]
    moved = sum(math.prod(a.shape) * a.dtype.itemsize for a in arrays + shapes)
    return pl.pallas_call(
        kernel,
        name=name,
        out_shape=shapes,
        in_specs=[place for _, place in args],
        out_specs=[place for _, _, place in outs],
        scratch_shapes=list(scratch),
        compiler_params=pltpu.CompilerParams(vmem_limit_bytes=grant),
        cost_estimate=pl.CostEstimate(flops=flops, bytes_accessed=moved, transcendentals=0),
    )(*arrays)


def on_device(
    features,
    tile_columns,
    tile_values,
    send_rows,
    send_count,
    ghost_target,
    query_rows,
    positive_cand,
    negative_rows,
    weight_self,
    weight_neigh,
):
    nodes, width = features.shape
    peers, slots = send_rows.shape[1:]
    total = peers * slots
    queries = query_rows.shape[1]
    negatives = negative_rows.shape[1]
    groups = lax.axis_size("group")
    others = groups - 1
    candidates = negatives * groups
    chips = peers // 2
    rows = 2 * width // peers
    half = chips // 2
    columns = width // groups
    grant = min(8 * groups, 56) << 20
    group = lax.axis_index("group").astype(jnp.int32)
    core = (lax.axis_index("dom") & 1).astype(jnp.int32)

    def of_others(own):
        return [
            lax.ppermute(own, "group", [((g + k) % groups, g) for g in range(groups)])
            for k in range(1, groups)
        ]

    id_rows = 16
    outgoing, joined = call(
        pack_kernel,
        "pack",
        [((peers, slots, width), BF16, HBM), ((nodes + id_rows, width), BF16, HBM)],
        [
            (a, HBM)
            for a in (
                send_rows, send_count, features, query_rows, positive_cand, negative_rows
            )
        ],
        flops=2 * total * nodes * width,
        scratch=[
            pltpu.VMEM(send_rows.shape, jnp.int32),
            pltpu.VMEM(send_count.shape, jnp.int32),
            pltpu.VMEM(features.shape, BF16),
            pltpu.VMEM(query_rows.shape, jnp.int32),
            pltpu.VMEM(positive_cand.shape, jnp.int32),
            pltpu.VMEM(negative_rows.shape, jnp.int32),
            pltpu.VMEM((peers, slots, width), BF16),
            pltpu.VMEM((id_rows, width), F32),
            pltpu.VMEM((id_rows, width), BF16),
            pltpu.SemaphoreType.DMA((10,)),
        ],
        grant=None,
    )
    received = lax.all_to_all(
        outgoing, "dom", split_axis=0, concat_axis=0, tiled=True
    ).reshape(total, width)

    joined = [joined] + of_others(joined)
    local, degree = call(
        local_kernel,
        "local",
        [((nodes, width), F32, VMEM), ((nodes, 128 + total), F32, VMEM)],
        [(tile_columns, SMEM), (tile_values, VMEM), (features, VMEM), (ghost_target, VMEM)],
        flops=2 * nodes * width * tile_values.shape[2] * tile_values.shape[3],
        grant=grant,
    )
    first, last = nodes // 2, nodes - nodes // 2
    head, tail = (
        call(
            functools.partial(aggregate_kernel, start),
            "aggregate",
            [((count, width), BF16, VMEM)],
            [(a, VMEM) for a in (received, local, degree)],
            flops=2 * count * total * width,
        )[0]
        for start, count in ((0, first), (first, last))
    )
    other_heads, other_tails = of_others(head), of_others(tail)
    node_turned = ((half, 2, rows, nodes), BF16, VMEM)
    core, group_place = core.reshape(1), (group.reshape(1), SMEM)
    embeds_out, embeds, part, scale, turned, pair, rest, hot, *made = call(
        functools.partial(embed_kernel, groups, (queries, negatives)),
        "embed",
        [
            ((nodes, width), BF16, HBM),
            ((nodes, width), BF16, VMEM),
            ((nodes, columns), F32, VMEM),
            ((nodes, 128), F32, VMEM),
            node_turned,
            ((candidates, groups * nodes), F32, VMEM),
            ((candidates, groups * nodes), F32, VMEM),
            ((candidates, groups * nodes), BF16, VMEM),
        ]
        + [((nodes, width), F32, VMEM)] * others
        + [node_turned] * groups,
        [group_place]
        + [(a, VMEM) for a in (head, tail, weight_self, weight_neigh, *joined)],
        flops=2 * nodes * width * width * groups,
        scratch=[pltpu.SemaphoreType.DMA],
        grant=grant,
    )
    x_turned, *features_turned = made[others:]
    pres = made[:others]
    ahead = call(
        ahead_kernel,
        "ahead",
        [
            ((first, columns), F32, VMEM),
            ((first, width), BF16, VMEM),
            ((first, 128), F32, VMEM),
            ((half, 2, rows, first), BF16, VMEM),
        ]
        * others,
        [group_place, (weight_neigh, VMEM)]
        + [(a, VMEM) for pair_of in zip(other_heads, pres) for a in pair_of],
        flops=2 * first * width * width,
        grant=grant,
    )
    members = []
    for n in range(others):
        members += [other_tails[n], pres[n], features_turned[n], *ahead[4 * n : 4 * n + 4]]
    send, *made = call(
        functools.partial(gradient_kernel, queries),
        "gradient",
        [((chips, rows, columns), BF16, VMEM)]
        + [((nodes, columns), BF16, VMEM)] * groups
        + [((half, 2, rows, last), BF16, VMEM)] * others,
        [(core, SMEM), group_place]
        + [
            (a, VMEM)
            for a in (
                weight_neigh,
                embeds,
                part,
                scale,
                pair,
                rest,
                hot,
                x_turned,
                turned,
                *members,
            )
        ],
        flops=2 * nodes * width * width,
        grant=grant,
    )
    pieces = [turned]
    for n in range(others):
        pieces += [ahead[4 * n + 3], made[groups + n]]
    (keep,) = call(
        functools.partial(keep_kernel, groups),
        "keep",
        [((chips, rows, columns), BF16, VMEM)],
        [(core, SMEM)]
        + [(a, VMEM) for a in (x_turned, *features_turned, *made[:groups], *pieces)],
        flops=2 * nodes * width * width,
        grant=grant,
    )

    swap = [(i, i ^ 1) for i in range(peers)]
    same_core = [[c + 2 * chip for chip in range(chips)] for c in range(2)]
    chip_sum = (keep.astype(F32) + lax.ppermute(send, "dom", swap).astype(F32)).astype(BF16)
    parts = lax.all_to_all(
        chip_sum,
        "dom",
        split_axis=0,
        concat_axis=0,
        axis_index_groups=same_core,
        tiled=True,
    )
    summed = jnp.sum(parts.astype(F32), axis=0).astype(BF16)
    if groups == 2:
        (other,) = of_others(summed)
        shard = jnp.where(
            group == 0,
            jnp.concatenate([summed, other], axis=1),
            jnp.concatenate([other, summed], axis=1),
        )
    else:
        shard = lax.all_gather(summed, "group", axis=1, tiled=True)
    return (embeds_out, shard)


def solution(mesh):
    placed = (
        P(("group", "dom"), None),
        P(("group", "dom"), None, None),
        P(("group", "dom"), None, None, None, None),
        P(("group", "dom"), None, None),
        P(("group", "dom"), None),
        P(("group", "dom"), None, None),
        P(("group", "dom"), None),
        P(("group", "dom"), None),
        P(("group", "dom"), None),
        P(),
        P(),
    )
    return jax.shard_map(
        on_device,
        mesh=mesh,
        in_specs=placed,
        out_specs=(P(("group", "dom"), None), P("dom", None)),
        check_vma=False,
    )
```
